128 devices in a mesh: dom: 128 (over y, z, x, core).
Axes of the slice: x: 4, y: 4, z: 4, core: 2. Of those that a mesh axis runs over, the one named last changes fastest.
Arguments:
- element_freedom_values: float32 [9, 20, 131072], P(None, None, 'dom'), may hold values from -6 to 6
- scaled_jacobian_matrices: float32 [3, 9, 9, 131072], P(None, None, None, 'dom'), may hold values from -2 to 2
- outward_face_normals: float32 [4, 3, 131072], P(None, None, 'dom'), may hold values from -3 to 3
- largest_wave_speed: float32 [131072], P('dom'), may hold values from 0.5 to 2
- element_cluster_index: int32 [131072], P('dom'), may hold values 0 or 1
- element_new_slot: int32 [131072], P('dom'), may hold values from 0 to 147455, as said below
- neighbours: int32 [4, 131072], P(None, 'dom'), may hold values from 0 to 147199, as said below
- face_rotation_codes: int32 [4, 131072], P(None, 'dom'), may hold values from 0 to 11
- deriv_mats: float32 [3, 20, 20], replicated, may hold values from -1.25 to 1.25
- stiff_mats: float32 [3, 20, 20], replicated, may hold values from -1.25 to 1.25
- face_eval: float32 [12, 20, 16], replicated, may hold values from -1.25 to 1.25
- face_lift: float32 [4, 16, 20], replicated, may hold values from -1.5 to 1.5
Outputs:
- new_state: float32 [9, 20, 147456], P(None, None, 'dom')
The draws below stay inside these ranges and needn't reach their ends.
Inputs may be any that keep to these rules, and one draw needn't show every extreme that they name: `element_new_slot`: one to one into slots partition * 1152 + local slot. Element 896 + j of partition d either stays at its local index or, on partitions that shed work, goes with g = j div 16 to partition (d + max(g * 16, 1)) mod 128, local slot 1024 + g * 16 + j mod 16; a partition sheds all 128 such elements or none; elements below 896 stay. Partitions 0 and 127 receive all 8 groups. `neighbours`: each names an occupied slot whose local index is below 896, on the element's own partition after migration or on one at s partitions' distance, s in -4..4 or s = 64, cyclically; at most one face of an element lies off its partition; from the elements of one partition after migration at most 32 faces name any one other partition, and partition 0 is named by exactly 32 faces from each of the nine partitions at those distances.
All inputs are finite; a program needn't handle non-finite values. No bound on the sum of `element_cluster_index` on one device may be relied on, other than what follows from the above.
Results may differ from the reference program's by a relative error of at most 0.0001.
Values sent between devices are 32-bit elements; how exact they have to be, the bound alone decides.
A program may use at most 256 MiB of HBM per device.

```python
import math
import jax
import jax.numpy as jnp
from jax import lax

QUANTITY_COUNT = 9
BASIS_COUNT = 20
NQ = 16
NORDER = 4
GROUPS = 8
E_DEV = 1024
CSZ = 16
KEEP = 896
PARTITION_SLOTS = 1152
REQ = 32
NE = 131072
N_DOM = 128


def group_offsets():
    return jnp.maximum(jnp.arange(GROUPS) * (N_DOM // GROUPS), 1)


def shed_flags(key):
    flags = jax.random.randint(jax.random.fold_in(key, 11), (N_DOM,), 0, 2)
    sources = group_offsets()
    flags = flags.at[(0 - sources) % N_DOM].set(1)
    flags = flags.at[(N_DOM - 1 - sources) % N_DOM].set(1)
    return flags


def draw_element_new_slot(key, part):
    flags = shed_flags(key)
    element = jnp.arange(N_DOM * E_DEV)
    device = element // E_DEV
    local = element % E_DEV
    moved = jnp.maximum(local - KEEP, 0)
    member = moved // CSZ
    target = (device + group_offsets()[member]) % N_DOM
    slot = E_DEV + member * CSZ + moved % CSZ
    leaves = (flags[device] == 1) & (local >= KEEP)
    return jnp.where(leaves, target * PARTITION_SLOTS + slot, device * PARTITION_SLOTS + local).astype(jnp.int32)


def new_links(key):
    offsets = jnp.array([1, 2, 3, 4, -1, -2, -3, -4, N_DOM // 2])
    spread = 9
    counts = jax.random.randint(jax.random.fold_in(key, 21), (N_DOM, spread), 1, REQ + 1)
    counts = counts.at[(0 - offsets) % N_DOM, jnp.arange(spread)].set(REQ)
    orders = jax.vmap(lambda sub: jax.random.permutation(sub, KEEP))(jax.random.split(jax.random.fold_in(key, 22), N_DOM))
    roles = jnp.concatenate([orders, jnp.full((N_DOM, PARTITION_SLOTS - KEEP), spread * REQ)], axis=1)
    which = jnp.minimum(roles // REQ, spread - 1)
    within = roles % REQ
    device = jnp.arange(N_DOM)[:, None]
    remote = (roles < spread * REQ) & (within < jnp.take_along_axis(counts, which, axis=1))
    far_device = (device + offsets[which]) % N_DOM
    far_slot = jax.random.randint(jax.random.fold_in(key, 23), (N_DOM, PARTITION_SLOTS), 0, KEEP)
    near_slot = jax.random.randint(jax.random.fold_in(key, 24), (4, N_DOM, PARTITION_SLOTS), 0, KEEP)
    remote_face = jax.random.randint(jax.random.fold_in(key, 25), (N_DOM, PARTITION_SLOTS), 0, 4)
    linked = device[None] * PARTITION_SLOTS + near_slot
    far_link = far_device * PARTITION_SLOTS + far_slot
    use_far = (jnp.arange(4)[:, None, None] == remote_face[None]) & remote[None]
    linked = jnp.where(use_far, far_link[None], linked)
    linked = linked.at[0, 0, PARTITION_SLOTS - 1].set(0)
    linked = linked.at[0, N_DOM - 1, PARTITION_SLOTS - 1].set((N_DOM - 1) * PARTITION_SLOTS + KEEP - 1)
    return linked.reshape(4, N_DOM * PARTITION_SLOTS)


def draw_neighbours(key, part):
    return new_links(key)[:, draw_element_new_slot(key, part)].astype(jnp.int32)


def with_ends(values, key, smallest, high):
    longest = values.shape.index(max(values.shape))
    spots = []
    for shift in (0, 1):
        where = [jax.random.randint(jax.random.fold_in(key, axis), (), 0, length) for axis, length in enumerate(values.shape)]
        where[longest] = (where[longest] + shift) % values.shape[longest]
        spots.append(tuple(where))
    return values.at[spots[0]].set(smallest).at[spots[1]].set(high)


def block_levels(stream_key, extent, cuts, least, largest):
    factor_of = 1.0
    for position, blocks in cuts:
        heights = jax.random.uniform(jax.random.fold_in(jax.random.fold_in(stream_key, 6), position), (blocks,), jnp.float32, least / len(cuts), largest / len(cuts))
        factor_of = factor_of * jnp.repeat(jnp.exp(heights), extent[position] // blocks).reshape((-1,) + (1,) * (len(extent) - 1 - position))
    return factor_of


def normal_values(own_key, dims, deviation, reach, cuts=(), held_as=jnp.bfloat16):
    values = jax.random.normal(own_key, dims, jnp.float32) * deviation
    if len(cuts) > 0:
        values = block_levels(own_key, dims, cuts, -0.22, 0.18) * values
    return jnp.clip(values, min=-reach, max=reach).astype(held_as)


def setup_inputs(seed: int = 0) -> dict:
    arg_keys = jax.random.split(jax.random.key(seed), 13)
    return {
        "element_freedom_values": normal_values(arg_keys[0], (QUANTITY_COUNT, BASIS_COUNT, NE), 1.0, 6.0, ((2, 128),), jnp.float32),
        "scaled_jacobian_matrices": normal_values(arg_keys[1], (3, QUANTITY_COUNT, QUANTITY_COUNT, NE), QUANTITY_COUNT ** -0.5, 2.0, ((3, 128),), jnp.float32),
        "outward_face_normals": normal_values(arg_keys[2], (4, 3, NE), 0.5, 3.0, ((2, 128),), jnp.float32),
        "largest_wave_speed": jnp.clip(jnp.exp(math.log(2.0) - 1.3862944 * jax.random.uniform(arg_keys[3], (NE,), jnp.float32) ** block_levels(arg_keys[3], (NE,), ((0, 128),), -0.2, 0.2)), 0.5, 2.0),
        "element_cluster_index": with_ends((jax.random.randint(arg_keys[4], (NE,), 0, 2) < 1).astype(jnp.int32), jax.random.fold_in(arg_keys[4], 1), 0, 1),
        "element_new_slot": draw_element_new_slot(jax.random.fold_in(arg_keys[12], 71), 0),
        "neighbours": draw_neighbours(jax.random.fold_in(arg_keys[12], 71), 0),
        "face_rotation_codes": with_ends(jax.random.randint(arg_keys[7], (4, NE), 0, 12), jax.random.fold_in(arg_keys[7], 1), 0, 11).astype(jnp.int32),
        "deriv_mats": normal_values(arg_keys[8], (3, BASIS_COUNT, BASIS_COUNT), BASIS_COUNT ** -0.5, 1.25, (), jnp.float32),
        "stiff_mats": normal_values(arg_keys[9], (3, BASIS_COUNT, BASIS_COUNT), BASIS_COUNT ** -0.5, 1.25, (), jnp.float32),
        "face_eval": normal_values(arg_keys[10], (12, BASIS_COUNT, NQ), BASIS_COUNT ** -0.5, 1.25, (), jnp.float32),
        "face_lift": normal_values(arg_keys[11], (4, NQ, BASIS_COUNT), NQ ** -0.5, 1.5, (), jnp.float32),
    }


step_fast = 0.25
precise = lax.Precision.HIGHEST


def coefficients(lower, upper):
    return [(upper ** (degree + 1) - lower ** (degree + 1)) / math.factorial(degree + 1) for degree in range(NORDER)]


def predictor(present_state, element_jacobian_set, deriv_mats):
    series = [present_state]
    for degree in range(NORDER - 1):
        turned = jnp.einsum('qce,dcb->dqbe', series[-1], deriv_mats, precision=precise)
        series.append(-jnp.einsum('dpqe,dqbe->pbe', element_jacobian_set, turned, precision=precise))
    return series


def integrate(series, lower, upper):
    result = jnp.zeros_like(series[0])
    for factor, member in zip(coefficients(lower, upper), series):
        result = result + factor * member
    return result


def update(integral, outside, element_jacobian_set, scaled_normals, element_speeds, face_rotations, stiff_mats, face_eval, face_lift):
    turned = jnp.einsum('qce,dcb->dqbe', integral, stiff_mats, precision=precise)
    change = jnp.einsum('dpqe,dqbe->pbe', element_jacobian_set, turned, precision=precise)
    for which_face in range(4):
        inner = jnp.einsum('pbe,bn->pne', integral, face_eval[3 * which_face], precision=precise)
        picked = jnp.take(face_eval, face_rotations[which_face], axis=0)
        outer = jnp.einsum('pbe,ebn->pne', outside[which_face], picked, precision=precise)
        normal_star = jnp.einsum('de,dpqe->pqe', scaled_normals[which_face], element_jacobian_set, precision=precise)
        flux = 0.5 * jnp.einsum('pqe,qne->pne', normal_star, inner + outer, precision=precise) + 0.5 * element_speeds * (inner - outer)
        change = change - jnp.einsum('pne,nb->pbe', flux, face_lift[which_face], precision=precise)
    return change


def reference(element_freedom_values, scaled_jacobian_matrices, outward_face_normals, largest_wave_speed, element_cluster_index, element_new_slot, neighbours, face_rotation_codes, deriv_mats, stiff_mats, face_eval, face_lift):
    slot_count = PARTITION_SLOTS * N_DOM
    present_state = jnp.zeros((QUANTITY_COUNT, BASIS_COUNT, slot_count), jnp.float32).at[:, :, element_new_slot].set(element_freedom_values)
    element_jacobian_set = jnp.zeros((3, QUANTITY_COUNT, QUANTITY_COUNT, slot_count), jnp.float32).at[:, :, :, element_new_slot].set(scaled_jacobian_matrices)
    scaled_normals = jnp.zeros((4, 3, slot_count), jnp.float32).at[:, :, element_new_slot].set(outward_face_normals)
    element_speeds = jnp.zeros((slot_count,), jnp.float32).at[element_new_slot].set(largest_wave_speed)
    time_clusters = jnp.zeros((slot_count,), jnp.int32).at[element_new_slot].set(element_cluster_index)
    neighbour_links = jnp.zeros((4, slot_count), jnp.int32).at[:, element_new_slot].set(neighbours)
    face_rotations = jnp.zeros((4, slot_count), jnp.int32).at[:, element_new_slot].set(face_rotation_codes)

    def outside(data):
        return [data[:, :, neighbour_links[which_face]] for which_face in range(4)]

    def apply(integral, others):
        return update(integral, others, element_jacobian_set, scaled_normals, element_speeds, face_rotations, stiff_mats, face_eval, face_lift)

    fast = (time_clusters == 0)[None, None, :]
    series = predictor(present_state, element_jacobian_set, deriv_mats)
    first = integrate(series, 0.0, step_fast)
    slow_second = integrate(series, step_fast, 2.0 * step_fast)
    first_out = outside(first)
    midway = jnp.where(fast, present_state + apply(first, first_out), present_state)
    fast_second = integrate(predictor(midway, element_jacobian_set, deriv_mats), 0.0, step_fast)
    second = jnp.where(fast, fast_second, slow_second)
    second_out = outside(second)
    fast_end = midway + apply(second, second_out)
    total = first + second
    total_out = outside(total)
    slow_end = present_state + apply(total, total_out)
    return jnp.where(fast, fast_end, slow_end)
```

```python
import functools
import math

import jax
import jax.numpy as jnp
import numpy as np
from jax import lax
from jax.experimental import pallas as pl
from jax.experimental.pallas import tpu as pltpu
from jax.sharding import PartitionSpec as P

NORDER = 4
CSZ = 16
GROUPS = 8
E_DEV = 1024
KEEP = 896
PARTITION_SLOTS = 1152
REQ = 32
NQ = 16
QN = 9
BN = 20
LANES = 128
BLOCKS = PARTITION_SLOTS // LANES
KEPT_BLOCKS = KEEP // LANES
ROWS = 184
TAIL = 144
SLAB = 512
ASKS = 384
STEP = 0.25
F32 = jnp.float32
BF16 = jnp.bfloat16
MESH = pl.DeviceIdType.MESH


def coefficients(lower, upper):
    return [
        (upper ** (degree + 1) - lower ** (degree + 1)) / math.factorial(degree + 1)
        for degree in range(NORDER)
    ]


def halves(matrix):
    high = lax.reduce_precision(matrix, 8, 7)
    return high.astype(BF16), (matrix - high).astype(BF16)


def stacked(matrix):
    high, low = halves(matrix)
    return jnp.concatenate([high, high, low], axis=-1)


DUP = np.array(list(range(20)) + [16, 17, 18, 19])


def grouped(mats, many):
    turned = jnp.swapaxes(mats, 1, 2)[:, DUP, :]
    eye = jnp.eye(many, dtype=F32)
    blown = turned[:, None, :, None, :] * eye[None, :, None, :, None]
    rows = mats.shape[0] * many * 24
    main = blown[..., :16].reshape(rows, many * 16)
    tail = blown[..., 16:].reshape(rows, many * 4)
    parts = [main, tail]
    if many == 1:
        parts.append(jnp.zeros((rows, 12), F32))
    return jnp.concatenate(parts, axis=1)


def grouped_points(mats, many):
    turned = jnp.swapaxes(mats, 1, 2)[:, DUP, :]
    eye = jnp.eye(many, dtype=F32)
    blown = turned[:, None, :, None, :] * eye[None, :, None, :, None]
    return blown.reshape(mats.shape[0], many * 24, many * NQ)


def constants(deriv_mats, stiff_mats, face_eval, face_lift):
    own = jnp.einsum("fcn,fnb->fcb", face_eval[::3], face_lift, precision=lax.Precision.HIGHEST)
    full = jnp.concatenate([stiff_mats, jnp.sum(own, axis=0)[None]], axis=0)
    result = []
    for many in (4, 1):
        result.append(stacked(grouped(-deriv_mats, many)))
    for many in (4, 1):
        result.append(stacked(grouped(full, many)))
    for many in (4, 1):
        inside = stacked(grouped(0.5 * own, many)).reshape(4, many * 24, -1)
        beyond = stacked(grouped_points(0.5 * face_lift, many))
        result.append(jnp.concatenate([inside, beyond], axis=-1))
    table = jnp.pad(face_eval.reshape(12, BN * NQ).T, ((0, 0), (0, 4)))
    result.append(jnp.concatenate(halves(table), axis=1))
    return result


def dot(a, b):
    return jnp.dot(a, b, preferred_element_type=F32)


def dot_nt(a, b):
    return lax.dot_general(a, b, (((1,), (1,)), ((), ())), preferred_element_type=F32)


def split(value):
    high = value.astype(BF16)
    return high, (value - high.astype(F32)).astype(BF16)


def triple(value):
    high, low = split(value)
    return jnp.concatenate([high, low, high], axis=0)


def lanes_of(ref, first, many, start, size):
    parts = [ref[first + i, pl.ds(start, size), :] for i in range(many)]
    return parts[0] if many == 1 else jnp.concatenate(parts, axis=1)


def quad_rows(ref, first, many, group):
    if group < 2:
        main = lanes_of(ref, first, many, 64 * group, 64)
        tail = lanes_of(ref, first, many, TAIL + 16 * group, 16)
        return triple(jnp.concatenate([main, tail], axis=0))
    main = lanes_of(ref, first, many, 128, 16)
    tail = lanes_of(ref, first, many, TAIL + 32, 8)
    blank = jnp.zeros((8, main.shape[1]), F32)
    return triple(jnp.concatenate([main, tail, blank], axis=0))


def put(ref, first, many, start, value):
    for i in range(many):
        ref[first + i, pl.ds(start, value.shape[0]), :] = value[:, LANES * i : LANES * (i + 1)]


def in_pairs(body, blocks):
    def step(i, carry):
        body(2 * i, 2)
        return carry

    lax.fori_loop(0, blocks // 2, step, 0)
    if blocks % 2:
        body(blocks - 1, 1)


def kernel(
    count,
    x_ref,
    jac_hbm,
    normal_ref,
    speed_ref,
    cluster_ref,
    slot_ref,
    link_ref,
    turn_ref,
    pred4_ref,
    pred1_ref,
    stiff4_ref,
    stiff1_ref,
    face4_ref,
    face1_ref,
    table_ref,
    out_ref,
    jac,
    pairs,
    info,
    present,
    first,
    second,
    base,
    series,
    turned,
    faces,
    points,
    gathered,
    tables,
    sources,
    wanted,
    placed,
    arrived,
    pack,
    got,
    ask_out,
    ask_in,
    answer_out,
    answer_in,
    jac_sem,
    pack_send,
    pack_recv,
    ask_send,
    ask_recv,
    answer_send,
    answer_recv,
):
    me = lax.axis_index("dom")
    group_steps = [max(g * (count // GROUPS), 1) for g in range(GROUPS)]
    reach = [1, 2, 3, 4, count - 1, count - 2, count - 3, count - 4, count // 2]
    greeted = sorted(
        {s % count for s in group_steps} | {-s % count for s in group_steps} | {s % count for s in reach}
    )

    def device(step):
        return (lax.rem(me + (step % count), count),)

    barrier = pltpu.get_barrier_semaphore()
    for step in greeted:
        pl.semaphore_signal(barrier, inc=1, device_id=device(step), device_id_type=MESH)

    jac_copy = pltpu.make_async_copy(jac_hbm, jac.at[:, :, :, pl.ds(0, E_DEV)], jac_sem)
    jac_copy.start()

    answer_in[:, pl.ds(288, 96), :] = jnp.zeros((2, 96, 256), F32)

    def load_block(b, carry):
        at = pl.ds(pl.multiple_of(b * LANES, LANES), LANES)
        for q in range(QN):
            present[b, pl.ds(16 * q, 16), :] = x_ref[q, 0:16, at]
            present[b, pl.ds(TAIL + 4 * q, 4), :] = x_ref[q, 16:20, at]
        present[b, pl.ds(180, 4), :] = jnp.zeros((4, LANES), F32)
        for f in range(4):
            info[b, pl.ds(3 * f, 3), :] = normal_ref[f, :, at]
        info[b, pl.ds(12, 1), :] = speed_ref[:, at]
        info[b, pl.ds(13, 1), :] = cluster_ref[:, at].astype(F32)
        info[b, pl.ds(14, 4), :] = link_ref[:, at].astype(F32)
        info[b, pl.ds(18, 4), :] = turn_ref[:, at].astype(F32)
        info[b, pl.ds(22, 2), :] = jnp.ones((2, LANES), F32)
        return carry

    lax.fori_loop(0, 8, load_block, 0)
    lane = lax.broadcasted_iota(jnp.int32, (1, LANES), 1)
    leaves = slot_ref[:, KEEP:E_DEV] != me * PARTITION_SLOTS + KEEP + lane

    jac_copy.wait()
    pack[pl.ds(0, ROWS), :] = jnp.where(leaves, present[7], 0.0)
    pack[pl.ds(ROWS, 24), :] = jnp.where(leaves, info[7], 0.0)
    for d in range(3):
        for p in range(QN):
            pack[pl.ds(208 + 9 * (9 * d + p), 9), :] = jnp.where(
                leaves, jac[d, p, :, pl.ds(KEEP, LANES)], 0.0
            )
    pack[pl.ds(451, SLAB - 451), :] = jnp.zeros((SLAB - 451, LANES), F32)
    for i in range(SLAB // LANES):
        got[0, :, pl.ds(LANES * i, LANES)] = pack[pl.ds(LANES * i, LANES), :].T
    info[7, pl.ds(22, 1), :] = jnp.where(leaves, 0.0, 1.0)

    pl.semaphore_wait(barrier, len(greeted))

    moves = []
    for g, step in enumerate(group_steps):
        part = pl.ds(CSZ * g, CSZ)
        copy = pltpu.make_async_remote_copy(
            src_ref=got.at[0, part],
            dst_ref=got.at[1, part],
            send_sem=pack_send.at[g],
            recv_sem=pack_recv.at[g],
            device_id=device(step),
            device_id_type=MESH,
        )
        copy.start()
        moves.append(copy)

    def pair_block(b, carry):
        at = pl.ds(pl.multiple_of(b * LANES, LANES), LANES)
        low = lax.broadcasted_iota(jnp.int32, (8, LANES), 0) < 4
        for d in range(3):
            for q in range(QN):
                for i in range(5):
                    upper = jac[d, min(2 * i + 1, 8), q : q + 1, at]
                    pairs[b, 9 * d + q, i] = jnp.where(low, jac[d, 2 * i, q : q + 1, at], upper)
        return carry

    def turn(ref, first_block, many, four_ref, one_ref, kinds, target):
        for group in range(3):
            right = quad_rows(ref, first_block, many, group)
            result = dot(four_ref[...] if group < 2 else one_ref[...], right)
            size = 96 if group < 2 else 24
            for d in range(kinds):
                put(target, first_block, many, 216 * d + 96 * group, result[size * d : size * (d + 1)])

    def apply_jacobian(b, load_turned):
        at = pl.ds(pl.multiple_of(b * LANES, LANES), LANES)
        main = None
        tail = None
        for d in range(3):
            for q in range(QN):
                upper, lower = load_turned(d, q)
                column = jac[d, :, q : q + 1, at]
                one = column * upper[None]
                two = pairs[b, 9 * d + q] * lower[None]
                main = one if main is None else main + one
                tail = two if tail is None else tail + two
        return jnp.concatenate([main.reshape(TAIL, LANES), tail.reshape(40, LANES)], axis=0)

    def plain_turned(b):
        def load(d, q):
            value = turned[b, pl.ds(216 * d + 24 * q, 24), :]
            return value[0:16], value[16:24]

        return load

    to_first = coefficients(0.0, STEP)
    to_slow = coefficients(STEP, 2.0 * STEP)

    def predict(start, blocks, from_block, finish):
        for degree in range(NORDER - 1):
            source = start if degree == 0 else series.at[degree - 1]

            def product(b, many):
                turn(source, from_block + b, many, pred4_ref, pred1_ref, 3, turned)

            in_pairs(product, blocks)

            def step(i, carry):
                b = from_block + i
                value = apply_jacobian(b, plain_turned(b))
                if degree < NORDER - 2:
                    series[degree, b] = value
                else:
                    finish(b, [start[b], series[0, b], series[1, b], value])
                return carry

            lax.fori_loop(0, blocks, step, 0)

    def weighted(factors, members):
        total = factors[0] * members[0]
        for factor, member in zip(factors[1:], members[1:]):
            total = total + factor * member
        return total

    def finish_first(b, members):
        first[b] = weighted(to_first, members)
        second[b] = weighted(to_slow, members)

    lax.fori_loop(0, 8, pair_block, 0)
    predict(present, 8, 0, finish_first)

    for copy in moves:
        copy.wait()
    for i in range(SLAB // LANES):
        pack[pl.ds(LANES * i, LANES), :] = got[1, :, pl.ds(LANES * i, LANES)].T
    present[8] = pack[pl.ds(0, ROWS), :]
    info[8] = pack[pl.ds(ROWS, 24), :]
    for d in range(3):
        for p in range(QN):
            jac[d, p, :, pl.ds(E_DEV, LANES)] = pack[pl.ds(208 + 9 * (9 * d + p), 9), :]
    pair_block(8, 0)

    which = lax.broadcasted_iota(jnp.int32, (16, LANES), 0)
    near = jnp.where(which < 4, which + 1, count + 3 - which)
    wanted_step = jnp.where(which < 8, near, jnp.where(which == 8, count // 2, -7)).astype(F32)
    row_f = which.astype(F32)
    me_f = (jnp.zeros((1, LANES), jnp.int32) + me).astype(F32)
    sums = jnp.where(
        lax.broadcasted_iota(jnp.int32, (LANES, 2 * LANES), 0)
        < lax.broadcasted_iota(jnp.int32, (LANES, 2 * LANES), 1),
        1.0,
        0.0,
    ).astype(BF16)

    def owners(b):
        link = info[b, pl.ds(14, 4), :]
        owner = jnp.floor((link + 0.5) * (1.0 / PARTITION_SLOTS))
        local = link - owner * PARTITION_SLOTS
        away = jnp.where(owner != me_f, info[b, pl.ds(22, 1), :], 0.0) > 0.5
        return owner, local, away

    def scan(b, carry):
        running, asked = carry
        owner, local, away = owners(b)
        step = owner - me_f
        step = jnp.where(step < 0.0, step + count, step)
        step = jnp.max(jnp.where(away, step, -1.0), axis=0, keepdims=True)
        spot = jnp.max(jnp.where(away, local, 0.0), axis=0, keepdims=True)
        hit = wanted_step == step
        member = jnp.where(hit, 1.0, 0.0)
        both = dot(member.astype(BF16), sums)
        place = jnp.where(hit, 32.0 * row_f + running + both[:, :LANES], 0.0)
        found = jnp.sum(member, axis=0, keepdims=True)
        place = jnp.sum(place, axis=0, keepdims=True) - (1.0 - found) * 1.0
        high = jnp.floor(spot * 0.125)
        text = jnp.concatenate([high, spot - 8.0 * high, found, jnp.zeros((13, LANES), F32)], axis=0)
        rows = lax.broadcasted_iota(jnp.int32, (ASKS, LANES), 0).astype(F32)
        marks = jnp.where(rows == place, 1.0, 0.0).astype(BF16)
        placed[b] = marks
        asked = asked + dot_nt(text.astype(BF16), marks)
        return running + both[:, LANES:], asked

    _, asked = lax.fori_loop(
        0, BLOCKS, scan, (jnp.zeros((16, LANES), F32), jnp.zeros((16, ASKS), F32))
    )
    asked = jnp.where(asked[2:3] > 0.5, 8.0 * asked[0:1] + asked[1:2], -1.0)
    ask_out[...] = jnp.broadcast_to(asked, (8, ASKS))
    requests = []
    for i, step in enumerate(reach):
        copy = pltpu.make_async_remote_copy(
            src_ref=ask_out,
            dst_ref=ask_in.at[i],
            send_sem=ask_send.at[i],
            recv_sem=ask_recv.at[i],
            device_id=device(step),
            device_id_type=MESH,
        )
        copy.start()
        requests.append(copy)

    predict(present, 1, 8, finish_first)

    def table_block(b, carry):
        codes = info[b, pl.ds(18, 4), :]
        kinds = lax.broadcasted_iota(jnp.int32, (16, LANES), 0).astype(F32)
        marks = [jnp.where(kinds == codes[f : f + 1], 1.0, 0.0).astype(BF16) for f in range(4)]
        marks = jnp.concatenate(marks, axis=1)
        value = dot(table_ref[...], jnp.concatenate([marks, marks], axis=0))
        for f in range(4):
            tables[4 * b + f] = value[:, LANES * f : LANES * (f + 1)]
        return carry

    lax.fori_loop(0, BLOCKS, table_block, 0)

    for copy in requests:
        copy.wait()
    asker = lax.broadcasted_iota(jnp.int32, (1, ASKS), 1) // REQ
    asked = jnp.full((1, ASKS), -1.0, F32)
    for i in range(len(reach)):
        asked = jnp.where(asker == i, ask_in[i, 0:1, :], asked)
    slots = lax.broadcasted_iota(jnp.int32, (KEEP, ASKS), 0).astype(F32)
    wanted[...] = jnp.where(slots == asked, 1.0, 0.0).astype(BF16)

    def exchange(field, turn_index):
        for b in range(KEPT_BLOCKS):
            high, low = split(field[b])
            sources[pl.ds(0, ROWS), pl.ds(LANES * b, LANES)] = high
            sources[pl.ds(192, ROWS), pl.ds(LANES * b, LANES)] = low
        answer = dot(sources[...], wanted[...])
        answer = answer[0:ROWS] + answer[192 : 192 + ROWS]
        answer = jnp.concatenate([answer, jnp.zeros((256 - ROWS, ASKS), F32)], axis=0)
        for i in range(ASKS // LANES):
            for j in range(2):
                answer_out[turn_index, pl.ds(LANES * i, LANES), pl.ds(LANES * j, LANES)] = answer[
                    LANES * j : LANES * (j + 1), LANES * i : LANES * (i + 1)
                ].T
        copies = []
        for i, step in enumerate(reach):
            part = pl.ds(REQ * i, REQ)
            copy = pltpu.make_async_remote_copy(
                src_ref=answer_out.at[turn_index, part],
                dst_ref=answer_in.at[turn_index, part],
                send_sem=answer_send.at[turn_index, i],
                recv_sem=answer_recv.at[turn_index, i],
                device_id=device(-step),
                device_id_type=MESH,
            )
            copy.start()
            copies.append(copy)
        return copies

    def local_gather(b, carry):
        owner, local, away = owners(b)
        slots = lax.broadcasted_iota(jnp.int32, (KEEP, LANES), 0).astype(F32)
        marks = [jnp.where(slots == local[f : f + 1], 1.0, 0.0).astype(BF16) for f in range(4)]
        value = dot(sources[...], jnp.concatenate(marks, axis=1))
        value = value[0:ROWS] + value[192 : 192 + ROWS]
        for f in range(4):
            gathered[4 * b + f] = value[:, LANES * f : LANES * (f + 1)]
        return carry

    def receive(turn_index, copies):
        for copy in copies:
            copy.wait()
        for i in range(ASKS // LANES):
            for j in range(2):
                block = answer_in[turn_index, pl.ds(LANES * i, LANES), pl.ds(LANES * j, LANES)].T
                if j == 1:
                    block = block[0 : ROWS - LANES]
                high, low = split(block)
                arrived[pl.ds(LANES * j, block.shape[0]), pl.ds(LANES * i, LANES)] = high
                arrived[pl.ds(192 + LANES * j, block.shape[0]), pl.ds(LANES * i, LANES)] = low

    def face_points(b, carry):
        owner, local, away = owners(b)
        value = dot_nt_placed(b)
        for f in range(4):
            gathered[4 * b + f] = jnp.where(away[f : f + 1], value, gathered[4 * b + f])
        return carry

    def dot_nt_placed(b):
        value = lax.dot_general(
            arrived[...], placed[b], (((1,), (0,)), ((), ())), preferred_element_type=F32
        )
        return value[0:ROWS] + value[192 : 192 + ROWS]

    def evaluate(i, carry):
        total = [None] * QN
        for c in range(BN):
            column = tables[i, pl.ds(NQ * c, NQ), :]
            for q in range(QN):
                row = 16 * q + c if c < 16 else TAIL + 4 * q + c - 16
                term = gathered[i, pl.ds(row, 1), :] * column
                total[q] = term if total[q] is None else total[q] + term
        for q in range(QN):
            points[i, pl.ds(NQ * q, NQ), :] = total[q]
        return carry

    def lift(field):
        def body(b, many):
            turn(field, b, many, stiff4_ref, stiff1_ref, 4, turned)
            for group in range(3):
                inside = quad_rows(field, b, many, group)
                size = 64 if group < 2 else 16
                for f in range(4):
                    parts = [points[4 * (b + i) + f, pl.ds(64 * group, size), :] for i in range(many)]
                    beyond = parts[0] if many == 1 else jnp.concatenate(parts, axis=1)
                    right = jnp.concatenate([inside, triple(beyond)], axis=0)
                    left = face4_ref[f] if group < 2 else face1_ref[f]
                    put(faces, b, many, 216 * f + 96 * group, dot(left, right))

        in_pairs(body, BLOCKS)

    low_half = lax.broadcasted_iota(jnp.int32, (8, LANES), 0) < 4

    def change_of(b):
        def load(d, q):
            value = turned[b, pl.ds(216 * d + 24 * q, 24), :]
            for f in range(4):
                value = value - info[b, pl.ds(3 * f + d, 1), :] * faces[b, pl.ds(216 * f + 24 * q, 24), :]
            return value[0:16], value[16:24]

        change = apply_jacobian(b, load)
        skew = []
        for q in range(QN):
            value = turned[b, pl.ds(648 + 24 * q, 24), :]
            for f in range(4):
                value = value - faces[b, pl.ds(216 * f + 24 * q, 24), :]
            skew.append(value)
        tails = [
            jnp.where(low_half, skew[2 * i][16:24], skew[min(2 * i + 1, 8)][16:24]) for i in range(5)
        ]
        skew = jnp.concatenate([s[0:16] for s in skew] + tails, axis=0)
        return change - info[b, pl.ds(12, 1), :] * skew

    def update(field, turn_index, finish):
        copies = exchange(field, turn_index)
        lax.fori_loop(0, BLOCKS, local_gather, 0)
        receive(turn_index, copies)
        lax.fori_loop(0, BLOCKS, face_points, 0)
        lax.fori_loop(0, 4 * BLOCKS, evaluate, 0)
        lift(field)

        def step(b, carry):
            finish(b, change_of(b))
            return carry

        lax.fori_loop(0, BLOCKS, step, 0)

    for half in range(2):
        arrived[pl.ds(192 * half + ROWS, 8), :] = jnp.zeros((8, ASKS), BF16)
        sources[pl.ds(192 * half + ROWS, 8), :] = jnp.zeros((8, KEEP), BF16)

    def finish_middle(b, change):
        base[b] = present[b] + change

    update(first, 0, finish_middle)

    def finish_second(b, members):
        quick = info[b, pl.ds(13, 1), :] < 0.5
        second[b] = jnp.where(quick, weighted(to_first, members), second[b])

    predict(base, BLOCKS, 0, finish_second)

    def finish_last(b, change):
        value = jnp.where(info[b, pl.ds(22, 1), :] > 0.5, base[b] + change, 0.0)
        at = pl.ds(pl.multiple_of(b * LANES, LANES), LANES)
        for q in range(QN):
            out_ref[q, 0:16, at] = value[16 * q : 16 * q + 16]
            out_ref[q, 16:20, at] = value[TAIL + 4 * q : TAIL + 4 * q + 4]

    update(second, 1, finish_last)


def per_device(
    count,
    element_freedom_values,
    scaled_jacobian_matrices,
    outward_face_normals,
    largest_wave_speed,
    element_cluster_index,
    element_new_slot,
    neighbours,
    face_rotation_codes,
    deriv_mats,
    stiff_mats,
    face_eval,
    face_lift,
):
    vmem = pl.BlockSpec(memory_space=pltpu.VMEM)
    consts = constants(deriv_mats, stiff_mats, face_eval, face_lift)
    return pl.pallas_call(
        functools.partial(kernel, count),
        out_shape=jax.ShapeDtypeStruct((QN, BN, PARTITION_SLOTS), F32),
        in_specs=[vmem, pl.BlockSpec(memory_space=pl.ANY)] + [vmem] * 13,
        out_specs=vmem,
        scratch_shapes=[
            pltpu.VMEM((3, QN, QN, PARTITION_SLOTS), F32),
            pltpu.VMEM((BLOCKS, 27, 5, 8, LANES), F32),
            pltpu.VMEM((BLOCKS, 24, LANES), F32),
            pltpu.VMEM((BLOCKS, ROWS, LANES), F32),
            pltpu.VMEM((BLOCKS, ROWS, LANES), F32),
            pltpu.VMEM((BLOCKS, ROWS, LANES), F32),
            pltpu.VMEM((BLOCKS, ROWS, LANES), F32),
            pltpu.VMEM((2, BLOCKS, ROWS, LANES), F32),
            pltpu.VMEM((BLOCKS, 864, LANES), F32),
            pltpu.VMEM((BLOCKS, 864, LANES), F32),
            pltpu.VMEM((4 * BLOCKS, TAIL, LANES), F32),
            pltpu.VMEM((4 * BLOCKS, ROWS, LANES), F32),
            pltpu.VMEM((4 * BLOCKS, BN * NQ, LANES), F32),
            pltpu.VMEM((384, KEEP), BF16),
            pltpu.VMEM((KEEP, ASKS), BF16),
            pltpu.VMEM((BLOCKS, ASKS, LANES), BF16),
            pltpu.VMEM((384, ASKS), BF16),
            pltpu.VMEM((SLAB, LANES), F32),
            pltpu.VMEM((2, LANES, SLAB), F32),
            pltpu.VMEM((8, ASKS), F32),
            pltpu.VMEM((9, 8, ASKS), F32),
            pltpu.VMEM((2, ASKS, 256), F32),
            pltpu.VMEM((2, ASKS, 256), F32),
            pltpu.SemaphoreType.DMA,
            pltpu.SemaphoreType.DMA((GROUPS,)),
            pltpu.SemaphoreType.DMA((GROUPS,)),
            pltpu.SemaphoreType.DMA((9,)),
            pltpu.SemaphoreType.DMA((9,)),
            pltpu.SemaphoreType.DMA((2, 9)),
            pltpu.SemaphoreType.DMA((2, 9)),
        ],
        compiler_params=pltpu.CompilerParams(
            collective_id=0, has_side_effects=True, vmem_limit_bytes=60 << 20
        ),
    )(
        element_freedom_values,
        scaled_jacobian_matrices,
        outward_face_normals,
        largest_wave_speed[None],
        element_cluster_index[None],
        element_new_slot[None],
        neighbours,
        face_rotation_codes,
        *consts,
    )


def solution(mesh):
    placed = (
        P(None, None, "dom"),
        P(None, None, None, "dom"),
        P(None, None, "dom"),
        P("dom"),
        P("dom"),
        P("dom"),
        P(None, "dom"),
        P(None, "dom"),
        P(),
        P(),
        P(),
        P(),
    )
    return jax.shard_map(
        functools.partial(per_device, mesh.shape["dom"]),
        mesh=mesh,
        in_specs=placed,
        out_specs=P(None, None, "dom"),
        check_vma=False,
    )
```

```python
import functools
import math

import jax
import jax.numpy as jnp
from jax import lax
from jax.experimental import pallas as pl
from jax.experimental.pallas import tpu as pltpu
from jax.sharding import PartitionSpec as P

NORDER = 4
CSZ = 16
GROUPS = 8
E_DEV = 1024
KEEP = 896
PARTITION_SLOTS = 1152
REQ = 32
NQ = 16
QN = 9
BN = 20
LANES = 128
BLOCKS = PARTITION_SLOTS // LANES
KEPT_BLOCKS = KEEP // LANES
ROWS = 184
TAIL = 144
SLAB = 512
ASKS = 384
STEP = 0.25
F32 = jnp.float32
BF16 = jnp.bfloat16
MESH = pl.DeviceIdType.MESH


def coefficients(lower, upper):
    return [
        (upper ** (degree + 1) - lower ** (degree + 1)) / math.factorial(degree + 1)
        for degree in range(NORDER)
    ]


def dot(a, b):
    return jnp.dot(a, b, preferred_element_type=F32)


def dot_nt(a, b):
    return lax.dot_general(a, b, (((1,), (1,)), ((), ())), preferred_element_type=F32)


def split(value):
    high = value.astype(BF16)
    return high, (value - high.astype(F32)).astype(BF16)


def triple(value):
    high, low = split(value)
    return jnp.concatenate([high, low, high], axis=0)


def lanes_of(ref, first, many, start, size):
    parts = [ref[first + i, pl.ds(start, size), :] for i in range(many)]
    return parts[0] if many == 1 else jnp.concatenate(parts, axis=1)


def quad_rows(ref, first, many, group):
    if group < 2:
        main = lanes_of(ref, first, many, 64 * group, 64)
        tail = lanes_of(ref, first, many, TAIL + 16 * group, 16)
        return triple(jnp.concatenate([main, tail], axis=0))
    main = lanes_of(ref, first, many, 128, 16)
    tail = lanes_of(ref, first, many, TAIL + 32, 8)
    blank = jnp.zeros((8, main.shape[1]), F32)
    return triple(jnp.concatenate([main, tail, blank], axis=0))


def put(ref, first, many, start, value):
    for i in range(many):
        ref[first + i, pl.ds(start, value.shape[0]), :] = value[:, LANES * i : LANES * (i + 1)]


def one_hot(test):
    return jnp.where(test, 1.0, 0.0).astype(BF16)


def grid_of(rows, columns):
    shape = (rows, columns)
    return lax.broadcasted_iota(jnp.int32, shape, 0), lax.broadcasted_iota(jnp.int32, shape, 1)


def band(value, width):
    return sum(jnp.where(value >= width * i, 1, 0) for i in range(1, 4))


def f32_split(value):
    high = value.astype(BF16).astype(F32)
    return high, value - high


def build_constants(deriv_ref, stiff_ref, eval_ref, lift_ref, pred4, pred1, stiff4, stiff1, lift4, lift1, table):
    r, c = grid_of(24, BN)
    expand = one_hot((r == c) | ((r == c + 4) & (r >= BN)))

    def columns(depth, width, section, code):
        r, j = grid_of(depth, 3 * width)
        which = band(j, width)
        hit = code(j - width * which) == r
        return one_hot(hit & (which < 2)), one_hot(hit & (which == 2)), section

    four = columns(BN, 80, None, lambda j: jnp.where(j < 64, j & 15, 16 + (j & 3)))
    one = columns(BN, 32, None, lambda j: j)
    four_points = columns(NQ, 64, None, lambda j: j & 15)
    one_points = columns(NQ, 16, None, lambda j: j)

    def same(rows, height, width, owner):
        i, j = grid_of(4 * height, 3 * width)
        return band(i, height) == owner(j - width * band(j, width))

    def owner80(j):
        return jnp.where(j < 64, j >> 4, (j - 64) >> 2)

    same24 = same(96, 24, 80, owner80)
    same16 = same(64, 16, 80, owner80)
    same_points = same(96, 24, 64, lambda j: j >> 4)

    def place(high, low, selectors):
        return dot(high.astype(BF16), selectors[0]) + dot(low.astype(BF16), selectors[1])

    def both(high, low, four_to, one_to, mask, selectors4, selectors1):
        tall = [jnp.concatenate([part] * 4, axis=0) for part in (high, low)]
        four_to[...] = jnp.where(mask, place(tall[0], tall[1], selectors4), 0.0).astype(BF16)
        one_to[...] = place(high, low, selectors1).astype(BF16)

    def rows_of(matrix):
        high, low = f32_split(matrix)
        return dot_nt(expand, high.astype(BF16)), dot_nt(expand, low.astype(BF16))

    for d in range(3):
        high, low = rows_of(-deriv_ref[d])
        both(high, low, pred4.at[pl.ds(96 * d, 96)], pred1.at[d], same24, four, one)
        high, low = rows_of(stiff_ref[d])
        both(high, low, stiff4.at[pl.ds(96 * d, 96)], stiff1.at[pl.ds(24 * d, 24)], same24, four, one)
    own = None
    for f in range(4):
        high, low = rows_of(lift_ref[f])
        values = eval_ref[3 * f]
        term = jnp.dot(high + low, values, precision=lax.Precision.HIGHEST, preferred_element_type=F32)
        own = term if own is None else own + term
        both(0.5 * high, 0.5 * low, lift4.at[f], lift1.at[f], same_points, four_points, one_points)
        high, low = f32_split(values)
        both(high, low, stiff4.at[pl.ds(384 + 64 * f, 64)], stiff1.at[pl.ds(96 + 16 * f, 16)], same16, four, one)
    high, low = f32_split(own)
    both(high, low, stiff4.at[pl.ds(288, 96)], stiff1.at[pl.ds(72, 24)], same24, four, one)

    r, j = grid_of(BN * NQ, BN)
    pick = one_hot((r >> 4) == j)
    r, j = grid_of(BN * NQ, 12 * NQ)
    level = (r & 15) == (j & 15)
    r, j = grid_of(12 * NQ, 32)
    kind_high, kind_low = one_hot((r >> 4) == j), one_hot((r >> 4) + 16 == j)
    high, low = f32_split(eval_ref[...].reshape(12 * NQ, BN))
    high = jnp.where(level, dot_nt(pick, high.astype(BF16)), 0.0)
    low = jnp.where(level, dot_nt(pick, low.astype(BF16)), 0.0)
    table[...] = (dot(high.astype(BF16), kind_high) + dot(low.astype(BF16), kind_low)).astype(BF16)


def kernel(
    count,
    x_ref,
    jac_hbm,
    normal_ref,
    speed_ref,
    cluster_ref,
    slot_ref,
    link_ref,
    turn_ref,
    deriv_ref,
    stiff_ref,
    eval_ref,
    lift_ref,
    out_ref,
    pred4,
    pred1,
    stiff4,
    stiff1,
    lift4,
    lift1,
    table,
    jac,
    pairs,
    info,
    present,
    first,
    second,
    base,
    series,
    turned,
    faces,
    points,
    gathered,
    tables,
    sources,
    marks,
    wanted,
    placed,
    arrived,
    pack,
    got,
    ask_out,
    ask_in,
    answer_out,
    answer_in,
    jac_sem,
    pack_send,
    pack_recv,
    ask_send,
    ask_recv,
    answer_send,
    answer_recv,
):
    me = lax.axis_index("dom")
    group_steps = [max(g * (count // GROUPS), 1) for g in range(GROUPS)]
    reach = [1, 2, 3, 4, count - 1, count - 2, count - 3, count - 4, count // 2]
    greeted = sorted(
        {s % count for s in group_steps} | {-s % count for s in group_steps} | {s % count for s in reach}
    )

    def device(step):
        return (lax.rem(me + (step % count), count),)

    barrier = pltpu.get_barrier_semaphore()
    for step in greeted:
        pl.semaphore_signal(barrier, inc=1, device_id=device(step), device_id_type=MESH)

    jac_copy = pltpu.make_async_copy(jac_hbm, jac.at[:, :, :, pl.ds(0, E_DEV)], jac_sem)
    jac_copy.start()

    answer_in[:, pl.ds(288, 96), :] = jnp.zeros((2, 96, 256), F32)
    for half in range(2):
        arrived[pl.ds(192 * half + ROWS, 8), :] = jnp.zeros((8, ASKS), BF16)
        sources[pl.ds(192 * half + ROWS, 8), :] = jnp.zeros((8, KEEP), BF16)

    def load_block(b, carry):
        at = pl.ds(pl.multiple_of(b * LANES, LANES), LANES)
        for q in range(QN):
            present[b, pl.ds(16 * q, 16), :] = x_ref[q, 0:16, at]
            present[b, pl.ds(TAIL + 4 * q, 4), :] = x_ref[q, 16:20, at]
        present[b, pl.ds(180, 4), :] = jnp.zeros((4, LANES), F32)
        for d in range(3):
            info[b, pl.ds(4 * d, 4), :] = normal_ref[d, :, at]
        info[b, pl.ds(12, 1), :] = speed_ref[:, at]
        info[b, pl.ds(13, 1), :] = cluster_ref[:, at].astype(F32)
        info[b, pl.ds(14, 4), :] = link_ref[:, at].astype(F32)
        info[b, pl.ds(18, 4), :] = turn_ref[:, at].astype(F32)
        info[b, pl.ds(22, 2), :] = jnp.ones((2, LANES), F32)
        return carry

    lax.fori_loop(0, 8, load_block, 0)
    lane = lax.broadcasted_iota(jnp.int32, (1, LANES), 1)
    leaves = slot_ref[:, KEEP:E_DEV] != me * PARTITION_SLOTS + KEEP + lane

    pack[pl.ds(0, ROWS), :] = jnp.where(leaves, present[7], 0.0)
    pack[pl.ds(ROWS, 24), :] = jnp.where(leaves, info[7], 0.0)
    pack[pl.ds(451, SLAB - 451), :] = jnp.zeros((SLAB - 451, LANES), F32)
    info[7, pl.ds(22, 1), :] = jnp.where(leaves, 0.0, 1.0)
    jac_copy.wait()
    for p in range(QN):
        for q in range(QN):
            pack[pl.ds(208 + 3 * (9 * p + q), 3), :] = jnp.where(
                leaves, jac[p, q, :, pl.ds(KEEP, LANES)], 0.0
            )
    for i in range(SLAB // LANES):
        got[0, :, pl.ds(LANES * i, LANES)] = pack[pl.ds(LANES * i, LANES), :].T

    pl.semaphore_wait(barrier, len(greeted))

    moves = []
    for g, step in enumerate(group_steps):
        part = pl.ds(CSZ * g, CSZ)
        copy = pltpu.make_async_remote_copy(
            src_ref=got.at[0, part],
            dst_ref=got.at[1, part],
            send_sem=pack_send.at[g],
            recv_sem=pack_recv.at[g],
            device_id=device(step),
            device_id_type=MESH,
        )
        copy.start()
        moves.append(copy)

    low_half = lax.broadcasted_iota(jnp.int32, (8, LANES), 0) < 4

    def pair_block(b, carry):
        at = pl.ds(pl.multiple_of(b * LANES, LANES), LANES)
        for d in range(3):
            for q in range(QN):
                for i in range(5):
                    upper = jac[min(2 * i + 1, 8), q, d : d + 1, at]
                    pairs[b, 9 * d + q, i] = jnp.where(low_half, jac[2 * i, q, d : d + 1, at], upper)
        return carry

    def turn(ref, first_block, many):
        for group in range(3):
            right = quad_rows(ref, first_block, many, group)
            if group < 2:
                result = dot(pred4[...], right)
                for d in range(3):
                    put(turned, first_block, many, 216 * d + 96 * group, result[96 * d : 96 * (d + 1)])
            else:
                result = dot(pred1[...].reshape(72, 96), right)
                for d in range(3):
                    put(turned, first_block, many, 216 * d + 192, result[24 * d : 24 * (d + 1)])

    def apply_jacobian(b, load_turned):
        at = pl.ds(pl.multiple_of(b * LANES, LANES), LANES)
        main = None
        tail = None
        for d in range(3):
            for q in range(QN):
                upper, lower = load_turned(d, q)
                column = jac[:, q, d : d + 1, at]
                one = column * upper[None]
                two = pairs[b, 9 * d + q] * lower[None]
                main = one if main is None else main + one
                tail = two if tail is None else tail + two
        return jnp.concatenate([main.reshape(TAIL, LANES), tail.reshape(40, LANES)], axis=0)

    def plain_turned(b):
        def load(d, q):
            value = turned[b, pl.ds(216 * d + 24 * q, 24), :]
            return value[0:16], value[16:24]

        return load

    to_first = coefficients(0.0, STEP)
    to_slow = coefficients(STEP, 2.0 * STEP)

    def pipelined(prepare, use, start, blocks):
        whole = blocks // 2

        def step(i, carry):
            use(start + 2 * i, 2)
            prepare(start + 2 * i + 2, 2)
            return carry

        lax.fori_loop(0, whole - 1, step, 0)
        if blocks % 2:
            use(start + 2 * whole - 2, 2)
            prepare(start + 2 * whole, 1)
            return lambda: use(start + 2 * whole, 1)
        return lambda: use(start + 2 * whole - 2, 2)

    def predict(field, start, blocks, finish):
        def source(degree):
            return field if degree == 0 else series.at[degree - 1]

        turn(source(0), start, 2)
        for degree in range(NORDER - 1):

            def use(b, many, degree=degree):
                for i in range(many):
                    value = apply_jacobian(b + i, plain_turned(b + i))
                    if degree < NORDER - 2:
                        series[degree, b + i] = value
                    else:
                        finish(b + i, [field[b + i], series[0, b + i], series[1, b + i], value])

            def prepare(b, many, degree=degree):
                turn(source(degree), b, many)

            last = pipelined(prepare, use, start, blocks)
            if degree < NORDER - 2 and blocks > 2:
                last()
                turn(source(degree + 1), start, 2)
            else:
                last()
                if degree < NORDER - 2:
                    turn(source(degree + 1), start, 2)

    def weighted(factors, members):
        total = factors[0] * members[0]
        for factor, member in zip(factors[1:], members[1:]):
            total = total + factor * member
        return total

    def finish_first(b, members):
        first[b] = weighted(to_first, members)
        second[b] = weighted(to_slow, members)

    build_constants(
        deriv_ref, stiff_ref, eval_ref, lift_ref, pred4, pred1, stiff4, stiff1, lift4, lift1, table
    )
    lax.fori_loop(0, 8, pair_block, 0)

    for copy in moves:
        copy.wait()
    for i in range(SLAB // LANES):
        pack[pl.ds(LANES * i, LANES), :] = got[1, :, pl.ds(LANES * i, LANES)].T
    present[8] = pack[pl.ds(0, ROWS), :]
    info[8] = pack[pl.ds(ROWS, 24), :]
    for p in range(QN):
        for q in range(QN):
            jac[p, q, :, pl.ds(E_DEV, LANES)] = pack[pl.ds(208 + 3 * (9 * p + q), 3), :]
    pair_block(8, 0)

    which = lax.broadcasted_iota(jnp.int32, (16, LANES), 0)
    near = jnp.where(which < 4, which + 1, count + 3 - which)
    wanted_step = jnp.where(which < 8, near, jnp.where(which == 8, count // 2, -7)).astype(F32)
    row_f = which.astype(F32)
    me_f = (jnp.zeros((1, LANES), jnp.int32) + me).astype(F32)
    r, c = grid_of(LANES, 2 * LANES)
    sums = one_hot(r < c)

    def owners(b):
        link = info[b, pl.ds(14, 4), :]
        owner = jnp.floor((link + 0.5) * (1.0 / PARTITION_SLOTS))
        local = link - owner * PARTITION_SLOTS
        away = jnp.where(owner != me_f, info[b, pl.ds(22, 1), :], 0.0) > 0.5
        return owner, local, away

    def scan(b, carry):
        running, asked = carry
        owner, local, away = owners(b)
        step = owner - me_f
        step = jnp.where(step < 0.0, step + count, step)
        step = jnp.max(jnp.where(away, step, -1.0), axis=0, keepdims=True)
        spot = jnp.max(jnp.where(away, local, 0.0), axis=0, keepdims=True)
        hit = wanted_step == step
        member = jnp.where(hit, 1.0, 0.0)
        prefix = dot(member.astype(BF16), sums)
        place = jnp.where(hit, 32.0 * row_f + running + prefix[:, :LANES], 0.0)
        found = jnp.sum(member, axis=0, keepdims=True)
        place = jnp.sum(place, axis=0, keepdims=True) - (1.0 - found)
        high = jnp.floor(spot * 0.125)
        text = jnp.concatenate([high, spot - 8.0 * high, found, jnp.zeros((13, LANES), F32)], axis=0)
        rows = lax.broadcasted_iota(jnp.int32, (ASKS, LANES), 0).astype(F32)
        chosen = one_hot(rows == place)
        placed[b] = chosen
        asked = asked + dot_nt(text.astype(BF16), chosen)
        return running + prefix[:, LANES:], asked

    _, asked = lax.fori_loop(
        0, BLOCKS, scan, (jnp.zeros((16, LANES), F32), jnp.zeros((16, ASKS), F32))
    )
    asked = jnp.where(asked[2:3] > 0.5, 8.0 * asked[0:1] + asked[1:2], -1.0)
    ask_out[...] = jnp.broadcast_to(asked, (8, ASKS))
    requests = []
    for i, step in enumerate(reach):
        copy = pltpu.make_async_remote_copy(
            src_ref=ask_out,
            dst_ref=ask_in.at[i],
            send_sem=ask_send.at[i],
            recv_sem=ask_recv.at[i],
            device_id=device(step),
            device_id_type=MESH,
        )
        copy.start()
        requests.append(copy)

    predict(present, 0, BLOCKS, finish_first)

    for copy in requests:
        copy.wait()
    asker = lax.broadcasted_iota(jnp.int32, (1, ASKS), 1) // REQ
    asked = jnp.full((1, ASKS), -1.0, F32)
    for i in range(len(reach)):
        asked = jnp.where(asker == i, ask_in[i, 0:1, :], asked)
    slots = lax.broadcasted_iota(jnp.int32, (KEEP, ASKS), 0).astype(F32)
    wanted[...] = one_hot(slots == asked)

    def exchange(field, turn_index):
        for b in range(KEPT_BLOCKS):
            high, low = split(field[b])
            sources[pl.ds(0, ROWS), pl.ds(LANES * b, LANES)] = high
            sources[pl.ds(192, ROWS), pl.ds(LANES * b, LANES)] = low
        answer = dot(sources[...], wanted[...])
        answer = answer[0:ROWS] + answer[192 : 192 + ROWS]
        answer = jnp.concatenate([answer, jnp.zeros((256 - ROWS, ASKS), F32)], axis=0)
        for i in range(ASKS // LANES):
            for j in range(2):
                answer_out[turn_index, pl.ds(LANES * i, LANES), pl.ds(LANES * j, LANES)] = answer[
                    LANES * j : LANES * (j + 1), LANES * i : LANES * (i + 1)
                ].T
        copies = []
        for i, step in enumerate(reach):
            part = pl.ds(REQ * i, REQ)
            copy = pltpu.make_async_remote_copy(
                src_ref=answer_out.at[turn_index, part],
                dst_ref=answer_in.at[turn_index, part],
                send_sem=answer_send.at[turn_index, i],
                recv_sem=answer_recv.at[turn_index, i],
                device_id=device(-step),
                device_id_type=MESH,
            )
            copy.start()
            copies.append(copy)
        return copies

    def table_block(b, carry):
        codes = info[b, pl.ds(18, 4), :]
        kinds = lax.broadcasted_iota(jnp.int32, (16, LANES), 0).astype(F32)
        chosen = jnp.concatenate([one_hot(kinds == codes[f : f + 1]) for f in range(4)], axis=1)
        value = dot(table[...], jnp.concatenate([chosen, chosen], axis=0))
        for f in range(4):
            tables[4 * b + f] = value[:, LANES * f : LANES * (f + 1)]
        return carry

    def mark_block(b, carry):
        _, local, _ = owners(b)
        slots = lax.broadcasted_iota(jnp.int32, (KEEP, LANES), 0).astype(F32)
        for f in range(4):
            marks[b, :, pl.ds(LANES * f, LANES)] = one_hot(slots == local[f : f + 1])
        return carry

    def receive(turn_index, copies):
        for copy in copies:
            copy.wait()
        for i in range(ASKS // LANES):
            for j in range(2):
                block = answer_in[turn_index, pl.ds(LANES * i, LANES), pl.ds(LANES * j, LANES)].T
                if j == 1:
                    block = block[0 : ROWS - LANES]
                high, low = split(block)
                arrived[pl.ds(LANES * j, block.shape[0]), pl.ds(LANES * i, LANES)] = high
                arrived[pl.ds(192 + LANES * j, block.shape[0]), pl.ds(LANES * i, LANES)] = low

    def gather(b):
        _, _, away = owners(b)
        value = dot(sources[...], marks[b])
        value = value[0:ROWS] + value[192 : 192 + ROWS]
        other = dot(arrived[...], placed[b])
        other = other[0:ROWS] + other[192 : 192 + ROWS]
        for f in range(4):
            gathered[4 * b + f] = jnp.where(
                away[f : f + 1], other, value[:, LANES * f : LANES * (f + 1)]
            )

    def evaluate(i):
        total = [points[i, pl.ds(NQ * q, NQ), :] for q in range(QN)]
        for c in range(BN):
            column = tables[i, pl.ds(NQ * c, NQ), :]
            for q in range(QN):
                row = 16 * q + c if c < 16 else TAIL + 4 * q + c - 16
                total[q] = total[q] + gathered[i, pl.ds(row, 1), :] * column
        for q in range(QN):
            points[i, pl.ds(NQ * q, NQ), :] = total[q]

    def inside(field, b, many):
        for group in range(3):
            right = quad_rows(field, b, many, group)
            tall = 96 if group < 2 else 24
            wide = 64 if group < 2 else 16
            result = dot(stiff4[...] if group < 2 else stiff1[...], right)
            for d in range(4):
                put(turned, b, many, 216 * d + 96 * group, result[tall * d : tall * (d + 1)])
            for f in range(4):
                part = result[4 * tall + wide * f : 4 * tall + wide * (f + 1)]
                for i in range(many):
                    points[4 * (b + i) + f, pl.ds(64 * group, wide), :] = part[
                        :, LANES * i : LANES * (i + 1)
                    ]

    def lift(b, many):
        for group in range(3):
            wide = 64 if group < 2 else 16
            for f in range(4):
                parts = [points[4 * (b + i) + f, pl.ds(64 * group, wide), :] for i in range(many)]
                right = parts[0] if many == 1 else jnp.concatenate(parts, axis=1)
                left = lift4[f] if group < 2 else lift1[f]
                put(faces, b, many, 216 * f + 96 * group, dot(left, triple(right)))

    def change_of(b):
        def load(d, q):
            value = turned[b, pl.ds(216 * d + 24 * q, 24), :]
            for f in range(4):
                value = value - info[b, pl.ds(4 * d + f, 1), :] * faces[b, pl.ds(216 * f + 24 * q, 24), :]
            return value[0:16], value[16:24]

        change = apply_jacobian(b, load)
        skew = []
        for q in range(QN):
            value = turned[b, pl.ds(648 + 24 * q, 24), :]
            for f in range(4):
                value = value - faces[b, pl.ds(216 * f + 24 * q, 24), :]
            skew.append(value)
        tails = [
            jnp.where(low_half, skew[2 * i][16:24], skew[min(2 * i + 1, 8)][16:24]) for i in range(5)
        ]
        skew = jnp.concatenate([s[0:16] for s in skew] + tails, axis=0)
        return change - info[b, pl.ds(12, 1), :] * skew

    def prepare_inside(field):
        def step(i, carry):
            inside(field, 2 * i, 2)
            return carry

        lax.fori_loop(0, BLOCKS // 2, step, 0)
        inside(field, BLOCKS - 1, 1)

    def update(turn_index, copies, finish):
        receive(turn_index, copies)
        gather(0)

        def step(b, carry):
            for f in range(4):
                evaluate(4 * b + f)
            gather(b + 1)
            return carry

        lax.fori_loop(0, BLOCKS - 1, step, 0)
        for f in range(4):
            evaluate(4 * (BLOCKS - 1) + f)
        lift(0, 2)

        def use(b, many):
            for i in range(many):
                finish(b + i, change_of(b + i))

        pipelined(lift, use, 0, BLOCKS)()

    copies = exchange(first, 0)
    lax.fori_loop(0, BLOCKS, table_block, 0)
    lax.fori_loop(0, BLOCKS, mark_block, 0)
    prepare_inside(first)

    def finish_middle(b, change):
        base[b] = present[b] + change

    update(0, copies, finish_middle)

    def finish_second(b, members):
        quick = info[b, pl.ds(13, 1), :] < 0.5
        second[b] = jnp.where(quick, weighted(to_first, members), second[b])

    predict(base, 0, KEPT_BLOCKS, finish_second)
    copies = exchange(second, 1)
    predict(base, KEPT_BLOCKS, 2, finish_second)
    prepare_inside(second)

    def finish_last(b, change):
        value = jnp.where(info[b, pl.ds(22, 1), :] > 0.5, base[b] + change, 0.0)
        at = pl.ds(pl.multiple_of(b * LANES, LANES), LANES)
        for q in range(QN):
            out_ref[q, 0:16, at] = value[16 * q : 16 * q + 16]
            out_ref[q, 16:20, at] = value[TAIL + 4 * q : TAIL + 4 * q + 4]

    update(1, copies, finish_last)


def per_device(
    count,
    element_freedom_values,
    scaled_jacobian_matrices,
    outward_face_normals,
    largest_wave_speed,
    element_cluster_index,
    element_new_slot,
    neighbours,
    face_rotation_codes,
    deriv_mats,
    stiff_mats,
    face_eval,
    face_lift,
):
    vmem = pl.BlockSpec(memory_space=pltpu.VMEM)
    return pl.pallas_call(
        functools.partial(kernel, count),
        out_shape=jax.ShapeDtypeStruct((QN, BN, PARTITION_SLOTS), F32),
        in_specs=[vmem, pl.BlockSpec(memory_space=pl.ANY)] + [vmem] * 10,
        out_specs=vmem,
        scratch_shapes=[
            pltpu.VMEM((288, 240), BF16),
            pltpu.VMEM((3, 24, 96), BF16),
            pltpu.VMEM((640, 240), BF16),
            pltpu.VMEM((160, 96), BF16),
            pltpu.VMEM((4, 96, 192), BF16),
            pltpu.VMEM((4, 24, 48), BF16),
            pltpu.VMEM((BN * NQ, 32), BF16),
            pltpu.VMEM((QN, QN, 3, PARTITION_SLOTS), F32),
            pltpu.VMEM((BLOCKS, 27, 5, 8, LANES), F32),
            pltpu.VMEM((BLOCKS, 24, LANES), F32),
            pltpu.VMEM((BLOCKS, ROWS, LANES), F32),
            pltpu.VMEM((BLOCKS, ROWS, LANES), F32),
            pltpu.VMEM((BLOCKS, ROWS, LANES), F32),
            pltpu.VMEM((BLOCKS, ROWS, LANES), F32),
            pltpu.VMEM((2, BLOCKS, ROWS, LANES), F32),
            pltpu.VMEM((BLOCKS, 864, LANES), F32),
            pltpu.VMEM((BLOCKS, 864, LANES), F32),
            pltpu.VMEM((4 * BLOCKS, TAIL, LANES), F32),
            pltpu.VMEM((4 * BLOCKS, ROWS, LANES), F32),
            pltpu.VMEM((4 * BLOCKS, BN * NQ, LANES), F32),
            pltpu.VMEM((384, KEEP), BF16),
            pltpu.VMEM((BLOCKS, KEEP, 4 * LANES), BF16),
            pltpu.VMEM((KEEP, ASKS), BF16),
            pltpu.VMEM((BLOCKS, ASKS, LANES), BF16),
            pltpu.VMEM((384, ASKS), BF16),
            pltpu.VMEM((SLAB, LANES), F32),
            pltpu.VMEM((2, LANES, SLAB), F32),
            pltpu.VMEM((8, ASKS), F32),
            pltpu.VMEM((9, 8, ASKS), F32),
            pltpu.VMEM((2, ASKS, 256), F32),
            pltpu.VMEM((2, ASKS, 256), F32),
            pltpu.SemaphoreType.DMA,
            pltpu.SemaphoreType.DMA((GROUPS,)),
            pltpu.SemaphoreType.DMA((GROUPS,)),
            pltpu.SemaphoreType.DMA((9,)),
            pltpu.SemaphoreType.DMA((9,)),
            pltpu.SemaphoreType.DMA((2, 9)),
            pltpu.SemaphoreType.DMA((2, 9)),
        ],
        compiler_params=pltpu.CompilerParams(
            collective_id=0, has_side_effects=True, vmem_limit_bytes=60 << 20
        ),
    )(
        element_freedom_values,
        jnp.transpose(scaled_jacobian_matrices, (1, 2, 0, 3)),
        jnp.transpose(outward_face_normals, (1, 0, 2)),
        largest_wave_speed[None],
        element_cluster_index[None],
        element_new_slot[None],
        neighbours,
        face_rotation_codes,
        deriv_mats,
        stiff_mats,
        jnp.swapaxes(face_eval, 1, 2),
        face_lift,
    )


def solution(mesh):
    placed = (
        P(None, None, "dom"),
        P(None, None, None, "dom"),
        P(None, None, "dom"),
        P("dom"),
        P("dom"),
        P("dom"),
        P(None, "dom"),
        P(None, "dom"),
        P(),
        P(),
        P(),
        P(),
    )
    return jax.shard_map(
        functools.partial(per_device, mesh.shape["dom"]),
        mesh=mesh,
        in_specs=placed,
        out_specs=P(None, None, "dom"),
        check_vma=False,
    )
```

```python
import functools
import math

import jax
import jax.numpy as jnp
from jax import lax
from jax.experimental import pallas as pl
from jax.experimental.pallas import tpu as pltpu
from jax.sharding import PartitionSpec as P

NORDER = 4
CSZ = 16
GROUPS = 8
E_DEV = 1024
KEEP = 896
PARTITION_SLOTS = 1152
REQ = 32
NQ = 16
QN = 9
BN = 20
LANES = 128
BLOCKS = PARTITION_SLOTS // LANES
KEPT_BLOCKS = KEEP // LANES
ROWS = 184
TAIL = 144
SLAB = 512
ASKS = 384
STEP = 0.25
F32 = jnp.float32
BF16 = jnp.bfloat16
MESH = pl.DeviceIdType.MESH


def coefficients(lower, upper):
    return [
        (upper ** (degree + 1) - lower ** (degree + 1)) / math.factorial(degree + 1)
        for degree in range(NORDER)
    ]


def dot(a, b):
    return jnp.dot(a, b, preferred_element_type=F32)


def dot_nt(a, b):
    return lax.dot_general(a, b, (((1,), (1,)), ((), ())), preferred_element_type=F32)


def split(value):
    high = value.astype(BF16)
    return high, (value - high.astype(F32)).astype(BF16)


def triple(value):
    high, low = split(value)
    return jnp.concatenate([high, low, high], axis=0)


def lanes_of(ref, first, start, size):
    return jnp.concatenate([ref[first + i, pl.ds(start, size), :] for i in range(2)], axis=1)


def quad_rows(ref, first, group):
    if group < 2:
        main = lanes_of(ref, first, 64 * group, 64)
        tail = lanes_of(ref, first, TAIL + 16 * group, 16)
        return triple(jnp.concatenate([main, tail], axis=0))
    main = lanes_of(ref, first, 128, 16)
    tail = lanes_of(ref, first, TAIL + 32, 8)
    blank = jnp.zeros((8, main.shape[1]), F32)
    return triple(jnp.concatenate([main, tail, blank], axis=0))


def put(ref, first, start, value):
    for i in range(2):
        ref[first + i, pl.ds(start, value.shape[0]), :] = value[:, LANES * i : LANES * (i + 1)]


def run(steps):
    for _ in steps:
        pass


def together(main, side, every):
    for count, _ in enumerate(main):
        if count % every == 0:
            next(side, None)
    run(side)


def one_hot(test):
    return jnp.where(test, 1.0, 0.0).astype(BF16)


def grid_of(rows, columns):
    shape = (rows, columns)
    return lax.broadcasted_iota(jnp.int32, shape, 0), lax.broadcasted_iota(jnp.int32, shape, 1)


def band(value, width):
    return sum(jnp.where(value >= width * i, 1, 0) for i in range(1, 4))


def f32_split(value):
    high = value.astype(BF16).astype(F32)
    return high, value - high


def build_constants(deriv_ref, stiff_ref, eval_ref, lift_ref, pred4, pred1, stiff4, stiff1, lift4, lift1, table):
    r, c = grid_of(24, BN)
    expand = one_hot((r == c) | ((r == c + 4) & (r >= BN)))

    def columns(depth, width, section, code):
        r, j = grid_of(depth, 3 * width)
        which = band(j, width)
        hit = code(j - width * which) == r
        return one_hot(hit & (which < 2)), one_hot(hit & (which == 2)), section

    four = columns(BN, 80, None, lambda j: jnp.where(j < 64, j & 15, 16 + (j & 3)))
    one = columns(BN, 32, None, lambda j: j)
    four_points = columns(NQ, 64, None, lambda j: j & 15)
    one_points = columns(NQ, 16, None, lambda j: j)

    def same(rows, height, width, owner):
        i, j = grid_of(4 * height, 3 * width)
        return band(i, height) == owner(j - width * band(j, width))

    def owner80(j):
        return jnp.where(j < 64, j >> 4, (j - 64) >> 2)

    same24 = same(96, 24, 80, owner80)
    same16 = same(64, 16, 80, owner80)
    same_points = same(96, 24, 64, lambda j: j >> 4)

    def place(high, low, selectors):
        return dot(high.astype(BF16), selectors[0]) + dot(low.astype(BF16), selectors[1])

    def both(high, low, four_to, one_to, mask, selectors4, selectors1):
        tall = [jnp.concatenate([part] * 4, axis=0) for part in (high, low)]
        four_to[...] = jnp.where(mask, place(tall[0], tall[1], selectors4), 0.0).astype(BF16)
        one_to[...] = place(high, low, selectors1).astype(BF16)

    def rows_of(matrix):
        high, low = f32_split(matrix)
        return dot_nt(expand, high.astype(BF16)), dot_nt(expand, low.astype(BF16))

    for d in range(3):
        high, low = rows_of(-deriv_ref[d])
        both(high, low, pred4.at[pl.ds(96 * d, 96)], pred1.at[d], same24, four, one)
        high, low = rows_of(stiff_ref[d])
        both(high, low, stiff4.at[pl.ds(96 * d, 96)], stiff1.at[pl.ds(24 * d, 24)], same24, four, one)
    own = None
    for f in range(4):
        high, low = rows_of(lift_ref[f])
        values = eval_ref[3 * f]
        term = jnp.dot(high + low, values, precision=lax.Precision.HIGHEST, preferred_element_type=F32)
        own = term if own is None else own + term
        both(0.5 * high, 0.5 * low, lift4.at[f], lift1.at[f], same_points, four_points, one_points)
        high, low = f32_split(values)
        both(high, low, stiff4.at[pl.ds(384 + 64 * f, 64)], stiff1.at[pl.ds(96 + 16 * f, 16)], same16, four, one)
    high, low = f32_split(own)
    both(high, low, stiff4.at[pl.ds(288, 96)], stiff1.at[pl.ds(72, 24)], same24, four, one)

    r, j = grid_of(BN * NQ, BN)
    pick = one_hot((r >> 4) == j)
    r, j = grid_of(BN * NQ, 12 * NQ)
    level = (r & 15) == (j & 15)
    r, j = grid_of(12 * NQ, 32)
    kind_high, kind_low = one_hot((r >> 4) == j), one_hot((r >> 4) + 16 == j)
    high, low = f32_split(eval_ref[...].reshape(12 * NQ, BN))
    high = jnp.where(level, dot_nt(pick, high.astype(BF16)), 0.0)
    low = jnp.where(level, dot_nt(pick, low.astype(BF16)), 0.0)
    table[...] = (dot(high.astype(BF16), kind_high) + dot(low.astype(BF16), kind_low)).astype(BF16)


def kernel(
    count,
    x_ref,
    jac_hbm,
    normal_ref,
    speed_ref,
    cluster_ref,
    slot_ref,
    link_ref,
    turn_ref,
    deriv_ref,
    stiff_ref,
    eval_ref,
    lift_ref,
    out_ref,
    pred4,
    pred1,
    stiff4,
    stiff1,
    lift4,
    lift1,
    table,
    jac,
    pairs,
    info,
    present,
    first,
    second,
    base,
    series0,
    series1,
    turned0,
    turned1,
    volume,
    faces0,
    faces1,
    points,
    gathered0,
    gathered1,
    tables,
    sources,
    marks,
    wanted,
    placed,
    arrived,
    pack,
    got,
    ask_out,
    ask_in,
    answer_out,
    answer_in,
    jac_sem,
    pack_send,
    pack_recv,
    ask_send,
    ask_recv,
    answer_send,
    answer_recv,
):
    me = lax.axis_index("dom")
    group_steps = [max(g * (count // GROUPS), 1) for g in range(GROUPS)]
    reach = [1, 2, 3, 4, count - 1, count - 2, count - 3, count - 4, count // 2]
    greeted = sorted(
        {s % count for s in group_steps} | {-s % count for s in group_steps} | {s % count for s in reach}
    )

    def device(step):
        return (lax.rem(me + (step % count), count),)

    barrier = pltpu.get_barrier_semaphore()
    for step in greeted:
        pl.semaphore_signal(barrier, inc=1, device_id=device(step), device_id_type=MESH)

    jac_copy = pltpu.make_async_copy(jac_hbm, jac.at[:, :, :, pl.ds(0, E_DEV)], jac_sem)
    jac_copy.start()

    answer_in[:, pl.ds(288, 96), :] = jnp.zeros((2, 96, 256), F32)
    for field in (present, first, second, base, series0, series1):
        field[BLOCKS] = jnp.zeros((ROWS, LANES), F32)
    info[BLOCKS] = jnp.zeros((24, LANES), F32)
    for half in range(2):
        arrived[pl.ds(192 * half + ROWS, 8), :] = jnp.zeros((8, ASKS), BF16)
        sources[pl.ds(192 * half + ROWS, 8), :] = jnp.zeros((8, KEEP), BF16)

    def load_block(b, carry):
        at = pl.ds(pl.multiple_of(b * LANES, LANES), LANES)
        for q in range(QN):
            present[b, pl.ds(16 * q, 16), :] = x_ref[q, 0:16, at]
            present[b, pl.ds(TAIL + 4 * q, 4), :] = x_ref[q, 16:20, at]
        present[b, pl.ds(180, 4), :] = jnp.zeros((4, LANES), F32)
        for d in range(3):
            info[b, pl.ds(4 * d, 4), :] = normal_ref[d, :, at]
        info[b, pl.ds(12, 1), :] = speed_ref[:, at]
        info[b, pl.ds(13, 1), :] = cluster_ref[:, at].astype(F32)
        info[b, pl.ds(14, 4), :] = link_ref[:, at].astype(F32)
        info[b, pl.ds(18, 4), :] = turn_ref[:, at].astype(F32)
        info[b, pl.ds(22, 2), :] = jnp.ones((2, LANES), F32)
        return carry

    lax.fori_loop(0, 8, load_block, 0)
    lane = lax.broadcasted_iota(jnp.int32, (1, LANES), 1)
    leaves = slot_ref[:, KEEP:E_DEV] != me * PARTITION_SLOTS + KEEP + lane

    pack[pl.ds(0, ROWS), :] = jnp.where(leaves, present[7], 0.0)
    pack[pl.ds(ROWS, 24), :] = jnp.where(leaves, info[7], 0.0)
    pack[pl.ds(451, SLAB - 451), :] = jnp.zeros((SLAB - 451, LANES), F32)
    info[7, pl.ds(22, 1), :] = jnp.where(leaves, 0.0, 1.0)
    jac_copy.wait()
    for p in range(QN):
        for q in range(QN):
            pack[pl.ds(208 + 3 * (9 * p + q), 3), :] = jnp.where(
                leaves, jac[p, q, :, pl.ds(KEEP, LANES)], 0.0
            )
    for i in range(SLAB // LANES):
        got[0, :, pl.ds(LANES * i, LANES)] = pack[pl.ds(LANES * i, LANES), :].T

    low_half = lax.broadcasted_iota(jnp.int32, (8, LANES), 0) < 4

    def pair_block(b, carry):
        at = pl.ds(pl.multiple_of(b * LANES, LANES), LANES)
        for d in range(3):
            for q in range(QN):
                for i in range(5):
                    upper = jac[min(2 * i + 1, 8), q, d : d + 1, at]
                    pairs[b, 9 * d + q, i] = jnp.where(low_half, jac[2 * i, q, d : d + 1, at], upper)
        return carry

    build_constants(
        deriv_ref, stiff_ref, eval_ref, lift_ref, pred4, pred1, stiff4, stiff1, lift4, lift1, table
    )
    lax.fori_loop(0, 8, pair_block, 0)

    pl.semaphore_wait(barrier, len(greeted))

    moves = []
    for g, step in enumerate(group_steps):
        part = pl.ds(CSZ * g, CSZ)
        copy = pltpu.make_async_remote_copy(
            src_ref=got.at[0, part],
            dst_ref=got.at[1, part],
            send_sem=pack_send.at[g],
            recv_sem=pack_recv.at[g],
            device_id=device(step),
            device_id_type=MESH,
        )
        copy.start()
        moves.append(copy)

    def turn(ref, b, target):
        for group in range(3):
            right = quad_rows(ref, b, group)
            yield
            tall = 96 if group < 2 else 24
            result = dot(pred4[...] if group < 2 else pred1[...].reshape(72, 96), right)
            yield
            for d in range(3):
                put(target, 0, 216 * d + 96 * group, result[tall * d : tall * (d + 1)])
                yield

    def apply_jacobian(b, load_turned):
        at = pl.ds(pl.multiple_of(b * LANES, LANES), LANES)
        main = None
        tail = None
        for d in range(3):
            for q in range(QN):
                upper, lower = load_turned(d, q)
                column = jac[:, q, d : d + 1, at]
                one = column * upper[None]
                two = pairs[b, 9 * d + q] * lower[None]
                main = one if main is None else main + one
                tail = two if tail is None else tail + two
                yield
        return jnp.concatenate([main.reshape(TAIL, LANES), tail.reshape(40, LANES)], axis=0)

    to_first = coefficients(0.0, STEP)
    to_slow = coefficients(STEP, 2.0 * STEP)

    def alternate(prepare, use, start, blocks, buffers, then, every):
        whole = (blocks + 1) // 2
        here, there = buffers
        double = (whole - 1) // 2

        def step(i, carry):
            b = start + 4 * i
            together(use(b, 2, here), prepare(b + 2, there), every)
            together(use(b + 2, 2, there), prepare(b + 4, here), every)
            return carry

        if double:
            lax.fori_loop(0, double, step, 0)
        if whole % 2 == 0:
            b = start + 4 * double
            together(use(b, 2, here), prepare(b + 2, there), every)
            here, there = there, here
        final = use(start + 2 * (whole - 1), 2 - blocks % 2, here)
        if whole == 1:
            run(final)
            run(then(there))
        else:
            together(final, then(there), every)
        return there, here

    def predict(field, start, blocks, finish):
        sources_of = [field, series0, series1]
        buffers = (turned0, turned1)
        run(turn(field, start, buffers[0]))
        for degree in range(NORDER - 1):

            def use(b, many, buffer, degree=degree):
                for i in range(many):

                    def load(d, q, i=i):
                        value = buffer[i, pl.ds(216 * d + 24 * q, 24), :]
                        return value[0:16], value[16:24]

                    value = yield from apply_jacobian(b + i, load)
                    if degree < NORDER - 2:
                        sources_of[degree + 1][b + i] = value
                    else:
                        finish(b + i, [field[b + i], series0[b + i], series1[b + i], value])

            def prepare(b, buffer, degree=degree):
                return turn(sources_of[degree], b, buffer)

            def then(buffer, degree=degree):
                if degree < NORDER - 2:
                    yield from turn(sources_of[degree + 1], start, buffer)

            buffers = alternate(prepare, use, start, blocks, buffers, then, 3)

    def weighted(factors, members):
        total = factors[0] * members[0]
        for factor, member in zip(factors[1:], members[1:]):
            total = total + factor * member
        return total

    def finish_first(b, members):
        first[b] = weighted(to_first, members)
        second[b] = weighted(to_slow, members)

    predict(present, 0, KEPT_BLOCKS, finish_first)

    for copy in moves:
        copy.wait()
    for i in range(SLAB // LANES):
        pack[pl.ds(LANES * i, LANES), :] = got[1, :, pl.ds(LANES * i, LANES)].T
    present[8] = pack[pl.ds(0, ROWS), :]
    info[8] = pack[pl.ds(ROWS, 24), :]
    for p in range(QN):
        for q in range(QN):
            jac[p, q, :, pl.ds(E_DEV, LANES)] = pack[pl.ds(208 + 3 * (9 * p + q), 3), :]
    pair_block(8, 0)

    which = lax.broadcasted_iota(jnp.int32, (16, LANES), 0)
    near = jnp.where(which < 4, which + 1, count + 3 - which)
    wanted_step = jnp.where(which < 8, near, jnp.where(which == 8, count // 2, -7)).astype(F32)
    row_f = which.astype(F32)
    me_f = (jnp.zeros((1, LANES), jnp.int32) + me).astype(F32)
    r, c = grid_of(LANES, 2 * LANES)
    sums = one_hot(r < c)

    def owners(b):
        link = info[b, pl.ds(14, 4), :]
        owner = jnp.floor((link + 0.5) * (1.0 / PARTITION_SLOTS))
        local = link - owner * PARTITION_SLOTS
        away = jnp.where(owner != me_f, info[b, pl.ds(22, 1), :], 0.0) > 0.5
        return owner, local, away

    def scan(b, carry):
        running, asked = carry
        owner, local, away = owners(b)
        step = owner - me_f
        step = jnp.where(step < 0.0, step + count, step)
        step = jnp.max(jnp.where(away, step, -1.0), axis=0, keepdims=True)
        spot = jnp.max(jnp.where(away, local, 0.0), axis=0, keepdims=True)
        hit = wanted_step == step
        member = jnp.where(hit, 1.0, 0.0)
        prefix = dot(member.astype(BF16), sums)
        place = jnp.where(hit, 32.0 * row_f + running + prefix[:, :LANES], 0.0)
        found = jnp.sum(member, axis=0, keepdims=True)
        place = jnp.sum(place, axis=0, keepdims=True) - (1.0 - found)
        high = jnp.floor(spot * 0.125)
        text = jnp.concatenate([high, spot - 8.0 * high, found, jnp.zeros((13, LANES), F32)], axis=0)
        rows = lax.broadcasted_iota(jnp.int32, (ASKS, LANES), 0).astype(F32)
        chosen = one_hot(rows == place)
        placed[b] = chosen
        asked = asked + dot_nt(text.astype(BF16), chosen)
        return running + prefix[:, LANES:], asked

    counted = (jnp.zeros((16, LANES), F32), jnp.zeros((16, ASKS), F32))
    for b in range(BLOCKS):
        counted = scan(b, counted)
    asked = counted[1]
    asked = jnp.where(asked[2:3] > 0.5, 8.0 * asked[0:1] + asked[1:2], -1.0)
    ask_out[...] = jnp.broadcast_to(asked, (8, ASKS))
    requests = []
    for i, step in enumerate(reach):
        copy = pltpu.make_async_remote_copy(
            src_ref=ask_out.at[:, pl.ds(LANES * (i // 4), LANES)],
            dst_ref=ask_in.at[i],
            send_sem=ask_send.at[i],
            recv_sem=ask_recv.at[i],
            device_id=device(step),
            device_id_type=MESH,
        )
        copy.start()
        requests.append(copy)

    predict(present, KEPT_BLOCKS, 2, finish_first)

    for copy in requests:
        copy.wait()
    asker = lax.broadcasted_iota(jnp.int32, (1, ASKS), 1) // REQ
    asked = jnp.full((1, ASKS), -1.0, F32)
    for i in range(len(reach)):
        answer = jnp.concatenate([ask_in[i, 0:1, :]] * (ASKS // LANES), axis=1)
        asked = jnp.where(asker == i, answer, asked)
    slots = lax.broadcasted_iota(jnp.int32, (KEEP, ASKS), 0).astype(F32)
    wanted[...] = one_hot(slots == asked)

    def exchange(field, turn_index):
        for b in range(KEPT_BLOCKS):
            high, low = split(field[b])
            sources[pl.ds(0, ROWS), pl.ds(LANES * b, LANES)] = high
            sources[pl.ds(192, ROWS), pl.ds(LANES * b, LANES)] = low
        answer = dot(sources[...], wanted[...])
        answer = answer[0:ROWS] + answer[192 : 192 + ROWS]
        answer = jnp.concatenate([answer, jnp.zeros((256 - ROWS, ASKS), F32)], axis=0)
        for i in range(ASKS // LANES):
            for j in range(2):
                answer_out[turn_index, pl.ds(LANES * i, LANES), pl.ds(LANES * j, LANES)] = answer[
                    LANES * j : LANES * (j + 1), LANES * i : LANES * (i + 1)
                ].T
        copies = []
        for i, step in enumerate(reach):
            part = pl.ds(REQ * i, REQ)
            copy = pltpu.make_async_remote_copy(
                src_ref=answer_out.at[turn_index, part],
                dst_ref=answer_in.at[turn_index, part],
                send_sem=answer_send.at[turn_index, i],
                recv_sem=answer_recv.at[turn_index, i],
                device_id=device(-step),
                device_id_type=MESH,
            )
            copy.start()
            copies.append(copy)
        return copies

    def table_block(b):
        codes = info[b, pl.ds(18, 4), :]
        kinds = lax.broadcasted_iota(jnp.int32, (16, LANES), 0).astype(F32)
        chosen = jnp.concatenate([one_hot(kinds == codes[f : f + 1]) for f in range(4)], axis=1)
        value = dot(table[...], jnp.concatenate([chosen, chosen], axis=0))
        for f in range(4):
            tables[4 * b + f] = value[:, LANES * f : LANES * (f + 1)]
            yield

    def mark_block(b):
        _, local, _ = owners(b)
        slots = lax.broadcasted_iota(jnp.int32, (KEEP, LANES), 0).astype(F32)
        for f in range(4):
            marks[b, :, pl.ds(LANES * f, LANES)] = one_hot(slots == local[f : f + 1])
            yield

    def receive(turn_index, copies):
        for copy in copies:
            copy.wait()
        for i in range(ASKS // LANES):
            for j in range(2):
                block = answer_in[turn_index, pl.ds(LANES * i, LANES), pl.ds(LANES * j, LANES)].T
                if j == 1:
                    block = block[0 : ROWS - LANES]
                high, low = split(block)
                arrived[pl.ds(LANES * j, block.shape[0]), pl.ds(LANES * i, LANES)] = high
                arrived[pl.ds(192 + LANES * j, block.shape[0]), pl.ds(LANES * i, LANES)] = low

    def gather(b, target):
        _, _, away = owners(b)
        other = dot(arrived[...], placed[b])
        other = other[0:ROWS] + other[192 : 192 + ROWS]
        yield
        for half in range(2):
            value = None
            for start in range(0, KEEP, 256):
                depth = pl.ds(start, min(256, KEEP - start))
                part = dot(sources[:, depth], marks[b, depth, pl.ds(256 * half, 256)])
                value = part if value is None else value + part
                yield
            value = value[0:ROWS] + value[192 : 192 + ROWS]
            for i in range(2):
                f = 2 * half + i
                target[f] = jnp.where(away[f : f + 1], other, value[:, LANES * i : LANES * (i + 1)])
                yield

    def evaluate(b, outer):
        for f in range(4):
            i = 4 * b + f
            total = [points[i, pl.ds(NQ * q, NQ), :] for q in range(QN)]
            for c in range(BN):
                column = tables[i, pl.ds(NQ * c, NQ), :]
                for q in range(QN):
                    row = 16 * q + c if c < 16 else TAIL + 4 * q + c - 16
                    total[q] = total[q] + outer[f, pl.ds(row, 1), :] * column
                yield
            for q in range(QN):
                points[i, pl.ds(NQ * q, NQ), :] = total[q]

    def inside(field, b):
        for group in range(3):
            right = quad_rows(field, b, group)
            yield
            tall = 96 if group < 2 else 24
            wide = 64 if group < 2 else 16
            result = dot(stiff4[...] if group < 2 else stiff1[...], right)
            yield
            for d in range(4):
                put(volume, b, 216 * d + 96 * group, result[tall * d : tall * (d + 1)])
            yield
            for f in range(4):
                part = result[4 * tall + wide * f : 4 * tall + wide * (f + 1)]
                for i in range(2):
                    points[4 * (b + i) + f, pl.ds(64 * group, wide), :] = part[
                        :, LANES * i : LANES * (i + 1)
                    ]
            yield

    def lift(b, target):
        for group in range(3):
            wide = 64 if group < 2 else 16
            for f in range(4):
                parts = [points[4 * (b + i) + f, pl.ds(64 * group, wide), :] for i in range(2)]
                right = triple(jnp.concatenate(parts, axis=1))
                yield
                left = lift4[f] if group < 2 else lift1[f]
                put(target, 0, 216 * f + 96 * group, dot(left, right))
                yield

    def change_of(b, face):
        def load(d, q):
            value = volume[b, pl.ds(216 * d + 24 * q, 24), :]
            for f in range(4):
                value = value - info[b, pl.ds(4 * d + f, 1), :] * face[pl.ds(216 * f + 24 * q, 24), :]
            return value[0:16], value[16:24]

        change = yield from apply_jacobian(b, load)
        skew = []
        for q in range(QN):
            value = volume[b, pl.ds(648 + 24 * q, 24), :]
            for f in range(4):
                value = value - face[pl.ds(216 * f + 24 * q, 24), :]
            skew.append(value)
            yield
        tails = [
            jnp.where(low_half, skew[2 * i][16:24], skew[min(2 * i + 1, 8)][16:24]) for i in range(5)
        ]
        skew = jnp.concatenate([s[0:16] for s in skew] + tails, axis=0)
        return change - info[b, pl.ds(12, 1), :] * skew

    def update(turn_index, copies, finish, later):
        receive(turn_index, copies)
        run(gather(0, gathered0))

        def step(i, carry):
            together(evaluate(2 * i, gathered0), gather(2 * i + 1, gathered1), 6)
            together(evaluate(2 * i + 1, gathered1), gather(2 * i + 2, gathered0), 6)
            return carry

        lax.fori_loop(0, BLOCKS // 2, step, 0)
        together(evaluate(BLOCKS - 1, gathered0), lift(0, faces0), 4)

        def use(b, many, face):
            for i in range(many):
                change = yield from change_of(b + i, face.at[i])
                finish(b + i, change)

        if not later:
            alternate(lift, use, 0, BLOCKS, (faces0, faces1), lambda buffer: iter(()), 3)
            return None
        rest = alternate(lift, use, 0, KEPT_BLOCKS, (faces0, faces1), lambda buffer: lift(KEPT_BLOCKS, buffer), 3)
        return use(KEPT_BLOCKS, 2, rest[0])

    copies = exchange(first, 0)

    def tables_and_inside(i):
        yield from table_block(2 * i)
        yield from table_block(2 * i + 1)
        yield from inside(first, 2 * i)

    def mark_pair(i):
        yield from mark_block(2 * i)
        yield from mark_block(2 * i + 1)

    def ready(i, carry):
        together(tables_and_inside(i), mark_pair(i), 2)
        return carry

    lax.fori_loop(0, BLOCKS // 2 + 1, ready, 0)

    def finish_middle(b, change):
        base[b] = present[b] + change

    rest = update(0, copies, finish_middle, True)

    def finish_second(b, members):
        quick = info[b, pl.ds(13, 1), :] < 0.5
        second[b] = jnp.where(quick, weighted(to_first, members), second[b])

    predict(base, 0, KEPT_BLOCKS, finish_second)
    copies = exchange(second, 1)
    run(rest)
    predict(base, KEPT_BLOCKS, 2, finish_second)

    def inside_pair(i, carry):
        run(inside(second, 2 * i))
        return carry

    lax.fori_loop(0, BLOCKS // 2 + 1, inside_pair, 0)

    def finish_last(b, change):
        value = jnp.where(info[b, pl.ds(22, 1), :] > 0.5, base[b] + change, 0.0)
        at = pl.ds(pl.multiple_of(b * LANES, LANES), LANES)
        for q in range(QN):
            out_ref[q, 0:16, at] = value[16 * q : 16 * q + 16]
            out_ref[q, 16:20, at] = value[TAIL + 4 * q : TAIL + 4 * q + 4]

    update(1, copies, finish_last, False)


def per_device(
    count,
    element_freedom_values,
    scaled_jacobian_matrices,
    outward_face_normals,
    largest_wave_speed,
    element_cluster_index,
    element_new_slot,
    neighbours,
    face_rotation_codes,
    deriv_mats,
    stiff_mats,
    face_eval,
    face_lift,
):
    vmem = pl.BlockSpec(memory_space=pltpu.VMEM)
    return pl.pallas_call(
        functools.partial(kernel, count),
        out_shape=jax.ShapeDtypeStruct((QN, BN, PARTITION_SLOTS), F32),
        in_specs=[vmem, pl.BlockSpec(memory_space=pl.ANY)] + [vmem] * 10,
        out_specs=vmem,
        scratch_shapes=[
            pltpu.VMEM((288, 240), BF16),
            pltpu.VMEM((3, 24, 96), BF16),
            pltpu.VMEM((640, 240), BF16),
            pltpu.VMEM((160, 96), BF16),
            pltpu.VMEM((4, 96, 192), BF16),
            pltpu.VMEM((4, 24, 48), BF16),
            pltpu.VMEM((BN * NQ, 32), BF16),
            pltpu.VMEM((QN, QN, 3, PARTITION_SLOTS), F32),
            pltpu.VMEM((BLOCKS, 27, 5, 8, LANES), F32),
            pltpu.VMEM((BLOCKS + 1, 24, LANES), F32),
            pltpu.VMEM((BLOCKS + 1, ROWS, LANES), F32),
            pltpu.VMEM((BLOCKS + 1, ROWS, LANES), F32),
            pltpu.VMEM((BLOCKS + 1, ROWS, LANES), F32),
            pltpu.VMEM((BLOCKS + 1, ROWS, LANES), F32),
            pltpu.VMEM((BLOCKS + 1, ROWS, LANES), F32),
            pltpu.VMEM((BLOCKS + 1, ROWS, LANES), F32),
            pltpu.VMEM((2, 648, LANES), F32),
            pltpu.VMEM((2, 648, LANES), F32),
            pltpu.VMEM((BLOCKS + 1, 864, LANES), F32),
            pltpu.VMEM((2, 864, LANES), F32),
            pltpu.VMEM((2, 864, LANES), F32),
            pltpu.VMEM((4 * BLOCKS + 4, TAIL, LANES), F32),
            pltpu.VMEM((4, ROWS, LANES), F32),
            pltpu.VMEM((4, ROWS, LANES), F32),
            pltpu.VMEM((4 * BLOCKS + 4, BN * NQ, LANES), F32),
            pltpu.VMEM((384, KEEP), BF16),
            pltpu.VMEM((BLOCKS + 1, KEEP, 4 * LANES), BF16),
            pltpu.VMEM((KEEP, ASKS), BF16),
            pltpu.VMEM((BLOCKS, ASKS, LANES), BF16),
            pltpu.VMEM((384, ASKS), BF16),
            pltpu.VMEM((SLAB, LANES), F32),
            pltpu.VMEM((2, LANES, SLAB), F32),
            pltpu.VMEM((8, ASKS), F32),
            pltpu.VMEM((9, 8, LANES), F32),
            pltpu.VMEM((2, ASKS, 256), F32),
            pltpu.VMEM((2, ASKS, 256), F32),
            pltpu.SemaphoreType.DMA,
            pltpu.SemaphoreType.DMA((GROUPS,)),
            pltpu.SemaphoreType.DMA((GROUPS,)),
            pltpu.SemaphoreType.DMA((9,)),
            pltpu.SemaphoreType.DMA((9,)),
            pltpu.SemaphoreType.DMA((2, 9)),
            pltpu.SemaphoreType.DMA((2, 9)),
        ],
        compiler_params=pltpu.CompilerParams(
            collective_id=0, has_side_effects=True, vmem_limit_bytes=56 << 20
        ),
    )(
        element_freedom_values,
        jnp.transpose(scaled_jacobian_matrices, (1, 2, 0, 3)),
        jnp.transpose(outward_face_normals, (1, 0, 2)),
        largest_wave_speed[None],
        element_cluster_index[None],
        element_new_slot[None],
        neighbours,
        face_rotation_codes,
        deriv_mats,
        stiff_mats,
        jnp.swapaxes(face_eval, 1, 2),
        face_lift,
    )


def solution(mesh):
    placed = (
        P(None, None, "dom"),
        P(None, None, None, "dom"),
        P(None, None, "dom"),
        P("dom"),
        P("dom"),
        P("dom"),
        P(None, "dom"),
        P(None, "dom"),
        P(),
        P(),
        P(),
        P(),
    )
    return jax.shard_map(
        functools.partial(per_device, mesh.shape["dom"]),
        mesh=mesh,
        in_specs=placed,
        out_specs=P(None, None, "dom"),
        check_vma=False,
    )
```

```python
import functools
import math

import jax
import jax.numpy as jnp
from jax import lax
from jax.experimental import pallas as pl
from jax.experimental.pallas import tpu as pltpu
from jax.sharding import PartitionSpec as P

NORDER = 4
CSZ = 16
GROUPS = 8
E_DEV = 1024
KEEP = 896
PARTITION_SLOTS = 1152
REQ = 32
NQ = 16
QN = 9
BN = 20
LANES = 128
BLOCKS = PARTITION_SLOTS // LANES
KEPT_BLOCKS = KEEP // LANES
ROWS = 184
TAIL = 144
SLAB = 512
ASKS = 384
STEP = 0.25
F32 = jnp.float32
BF16 = jnp.bfloat16
MESH = pl.DeviceIdType.MESH


def coefficients(lower, upper):
    return [
        (upper ** (degree + 1) - lower ** (degree + 1)) / math.factorial(degree + 1)
        for degree in range(NORDER)
    ]


def dot(a, b):
    return jnp.dot(a, b, preferred_element_type=F32)


def dot_nt(a, b):
    return lax.dot_general(a, b, (((1,), (1,)), ((), ())), preferred_element_type=F32)


def split(value):
    high = value.astype(BF16)
    return high, (value - high.astype(F32)).astype(BF16)


def triple(value):
    high, low = split(value)
    return jnp.concatenate([high, low, high], axis=0)


def lanes_of(ref, first, start, size):
    return jnp.concatenate([ref[first + i, pl.ds(start, size), :] for i in range(2)], axis=1)


def quad_rows(ref, first, group):
    if group < 2:
        main = lanes_of(ref, first, 64 * group, 64)
        tail = lanes_of(ref, first, TAIL + 16 * group, 16)
        return triple(jnp.concatenate([main, tail], axis=0))
    main = lanes_of(ref, first, 128, 16)
    tail = lanes_of(ref, first, TAIL + 32, 8)
    blank = jnp.zeros((8, main.shape[1]), F32)
    return triple(jnp.concatenate([main, tail, blank], axis=0))


def put(ref, first, start, value):
    for i in range(2):
        ref[first + i, pl.ds(start, value.shape[0]), :] = value[:, LANES * i : LANES * (i + 1)]


def run(steps):
    for _ in steps:
        pass


def together(main, side, every):
    for count, _ in enumerate(main):
        if count % every == 0:
            next(side, None)
    run(side)


def one_hot(test):
    return jnp.where(test, 1.0, 0.0).astype(BF16)


def grid_of(rows, columns):
    shape = (rows, columns)
    return lax.broadcasted_iota(jnp.int32, shape, 0), lax.broadcasted_iota(jnp.int32, shape, 1)


def band(value, width):
    return sum(jnp.where(value >= width * i, 1, 0) for i in range(1, 4))


def f32_split(value):
    high = value.astype(BF16).astype(F32)
    return high, value - high


def build_constants(deriv_ref, stiff_ref, eval_ref, lift_ref, pred4, pred1, stiff4, stiff1, lift4, lift1, table):
    r, c = grid_of(24, BN)
    expand = one_hot((r == c) | ((r == c + 4) & (r >= BN)))

    def columns(depth, width, section, code):
        r, j = grid_of(depth, 3 * width)
        which = band(j, width)
        hit = code(j - width * which) == r
        return one_hot(hit & (which < 2)), one_hot(hit & (which == 2)), section

    four = columns(BN, 80, None, lambda j: jnp.where(j < 64, j & 15, 16 + (j & 3)))
    one = columns(BN, 32, None, lambda j: j)
    four_points = columns(NQ, 64, None, lambda j: j & 15)
    one_points = columns(NQ, 16, None, lambda j: j)

    def same(rows, height, width, owner):
        i, j = grid_of(4 * height, 3 * width)
        return band(i, height) == owner(j - width * band(j, width))

    def owner80(j):
        return jnp.where(j < 64, j >> 4, (j - 64) >> 2)

    same24 = same(96, 24, 80, owner80)
    same16 = same(64, 16, 80, owner80)
    same_points = same(96, 24, 64, lambda j: j >> 4)

    def place(high, low, selectors):
        return dot(high.astype(BF16), selectors[0]) + dot(low.astype(BF16), selectors[1])

    def both(high, low, four_to, one_to, mask, selectors4, selectors1):
        tall = [jnp.concatenate([part] * 4, axis=0) for part in (high, low)]
        four_to[...] = jnp.where(mask, place(tall[0], tall[1], selectors4), 0.0).astype(BF16)
        one_to[...] = place(high, low, selectors1).astype(BF16)

    def rows_of(matrix):
        high, low = f32_split(matrix)
        return dot_nt(expand, high.astype(BF16)), dot_nt(expand, low.astype(BF16))

    for d in range(3):
        high, low = rows_of(-deriv_ref[d])
        both(high, low, pred4.at[pl.ds(96 * d, 96)], pred1.at[d], same24, four, one)
        high, low = rows_of(stiff_ref[d])
        both(high, low, stiff4.at[pl.ds(96 * d, 96)], stiff1.at[pl.ds(24 * d, 24)], same24, four, one)
    own = None
    for f in range(4):
        high, low = rows_of(lift_ref[f])
        values = eval_ref[3 * f]
        term = jnp.dot(high + low, values, precision=lax.Precision.HIGHEST, preferred_element_type=F32)
        own = term if own is None else own + term
        both(0.5 * high, 0.5 * low, lift4.at[f], lift1.at[f], same_points, four_points, one_points)
        high, low = f32_split(values)
        both(high, low, stiff4.at[pl.ds(384 + 64 * f, 64)], stiff1.at[pl.ds(96 + 16 * f, 16)], same16, four, one)
    high, low = f32_split(own)
    both(high, low, stiff4.at[pl.ds(288, 96)], stiff1.at[pl.ds(72, 24)], same24, four, one)

    r, j = grid_of(BN * NQ, BN)
    pick = one_hot((r >> 4) == j)
    r, j = grid_of(BN * NQ, 12 * NQ)
    level = (r & 15) == (j & 15)
    r, j = grid_of(12 * NQ, 32)
    kind_high, kind_low = one_hot((r >> 4) == j), one_hot((r >> 4) + 16 == j)
    high, low = f32_split(eval_ref[...].reshape(12 * NQ, BN))
    high = jnp.where(level, dot_nt(pick, high.astype(BF16)), 0.0)
    low = jnp.where(level, dot_nt(pick, low.astype(BF16)), 0.0)
    table[...] = (dot(high.astype(BF16), kind_high) + dot(low.astype(BF16), kind_low)).astype(BF16)


def kernel(
    count,
    x_ref,
    jac_hbm,
    normal_ref,
    speed_ref,
    cluster_ref,
    slot_ref,
    link_ref,
    turn_ref,
    deriv_ref,
    stiff_ref,
    eval_ref,
    lift_ref,
    out_ref,
    pred4,
    pred1,
    stiff4,
    stiff1,
    lift4,
    lift1,
    table,
    jac,
    pairs,
    info,
    present,
    first,
    second,
    base,
    series0,
    series1,
    turned0,
    turned1,
    volume,
    faces0,
    faces1,
    points,
    gathered0,
    gathered1,
    tables,
    sources,
    marks,
    wanted,
    placed,
    arrived,
    pack,
    got,
    ask_out,
    ask_in,
    answer_out,
    answer_in,
    jac_sem,
    pack_send,
    pack_recv,
    ask_send,
    ask_recv,
    answer_send,
    answer_recv,
):
    me = lax.axis_index("dom")
    group_steps = [max(g * (count // GROUPS), 1) for g in range(GROUPS)]
    reach = [1, 2, 3, 4, count - 1, count - 2, count - 3, count - 4, count // 2]
    greeted = sorted(
        {s % count for s in group_steps} | {-s % count for s in group_steps} | {s % count for s in reach}
    )

    def device(step):
        return (lax.rem(me + (step % count), count),)

    barrier = pltpu.get_barrier_semaphore()
    for step in greeted:
        pl.semaphore_signal(barrier, inc=1, device_id=device(step), device_id_type=MESH)

    jac_copy = pltpu.make_async_copy(jac_hbm, jac.at[:, :, :, pl.ds(0, E_DEV)], jac_sem)
    jac_copy.start()

    answer_in[:, pl.ds(288, 96), :] = jnp.zeros((2, 96, 256), F32)
    for field in (present, first, second, base, series0, series1):
        field[BLOCKS] = jnp.zeros((ROWS, LANES), F32)
    info[BLOCKS] = jnp.zeros((24, LANES), F32)
    for half in range(2):
        arrived[pl.ds(192 * half + ROWS, 8), :] = jnp.zeros((8, ASKS), BF16)
        sources[pl.ds(192 * half + ROWS, 8), :] = jnp.zeros((8, KEEP), BF16)

    def load_block(b, carry):
        at = pl.ds(pl.multiple_of(b * LANES, LANES), LANES)
        for q in range(QN):
            present[b, pl.ds(16 * q, 16), :] = x_ref[q, 0:16, at]
            present[b, pl.ds(TAIL + 4 * q, 4), :] = x_ref[q, 16:20, at]
        present[b, pl.ds(180, 4), :] = jnp.zeros((4, LANES), F32)
        for d in range(3):
            info[b, pl.ds(4 * d, 4), :] = normal_ref[d, :, at]
        info[b, pl.ds(12, 1), :] = speed_ref[:, at]
        info[b, pl.ds(13, 1), :] = cluster_ref[:, at].astype(F32)
        info[b, pl.ds(14, 4), :] = link_ref[:, at].astype(F32)
        info[b, pl.ds(18, 4), :] = turn_ref[:, at].astype(F32)
        info[b, pl.ds(22, 2), :] = jnp.ones((2, LANES), F32)
        return carry

    lax.fori_loop(0, 8, load_block, 0)
    lane = lax.broadcasted_iota(jnp.int32, (1, LANES), 1)
    leaves = slot_ref[:, KEEP:E_DEV] != me * PARTITION_SLOTS + KEEP + lane

    pack[pl.ds(0, ROWS), :] = jnp.where(leaves, present[7], 0.0)
    pack[pl.ds(ROWS, 24), :] = jnp.where(leaves, info[7], 0.0)
    pack[pl.ds(451, SLAB - 451), :] = jnp.zeros((SLAB - 451, LANES), F32)
    info[7, pl.ds(22, 1), :] = jnp.where(leaves, 0.0, 1.0)
    jac_copy.wait()
    for p in range(QN):
        for q in range(QN):
            pack[pl.ds(208 + 3 * (9 * p + q), 3), :] = jnp.where(
                leaves, jac[p, q, :, pl.ds(KEEP, LANES)], 0.0
            )
    for i in range(SLAB // LANES):
        got[0, :, pl.ds(LANES * i, LANES)] = pack[pl.ds(LANES * i, LANES), :].T

    low_half = lax.broadcasted_iota(jnp.int32, (8, LANES), 0) < 4

    def pair_block(b, carry):
        at = pl.ds(pl.multiple_of(b * LANES, LANES), LANES)
        for d in range(3):
            for q in range(QN):
                for i in range(5):
                    upper = jac[min(2 * i + 1, 8), q, d : d + 1, at]
                    pairs[b, 9 * d + q, i] = jnp.where(low_half, jac[2 * i, q, d : d + 1, at], upper)
        return carry

    build_constants(
        deriv_ref, stiff_ref, eval_ref, lift_ref, pred4, pred1, stiff4, stiff1, lift4, lift1, table
    )
    lax.fori_loop(0, 8, pair_block, 0)

    pl.semaphore_wait(barrier, len(greeted))

    moves = []
    for g, step in enumerate(group_steps):
        part = pl.ds(CSZ * g, CSZ)
        copy = pltpu.make_async_remote_copy(
            src_ref=got.at[0, part],
            dst_ref=got.at[1, part],
            send_sem=pack_send.at[g],
            recv_sem=pack_recv.at[g],
            device_id=device(step),
            device_id_type=MESH,
        )
        copy.start()
        moves.append(copy)

    def turn(ref, b, target):
        for group in range(3):
            right = quad_rows(ref, b, group)
            yield
            tall = 96 if group < 2 else 24
            result = dot(pred4[...] if group < 2 else pred1[...].reshape(72, 96), right)
            yield
            for d in range(3):
                put(target, 0, 216 * d + 96 * group, result[tall * d : tall * (d + 1)])
                yield

    def apply_jacobian(b, load_turned):
        at = pl.ds(pl.multiple_of(b * LANES, LANES), LANES)
        main = None
        tail = None
        for d in range(3):
            for q in range(QN):
                upper, lower = load_turned(d, q)
                column = jac[:, q, d : d + 1, at]
                one = column * upper[None]
                two = pairs[b, 9 * d + q] * lower[None]
                main = one if main is None else main + one
                tail = two if tail is None else tail + two
                yield
        return jnp.concatenate([main.reshape(TAIL, LANES), tail.reshape(40, LANES)], axis=0)

    to_first = coefficients(0.0, STEP)
    to_slow = coefficients(STEP, 2.0 * STEP)

    def alternate(prepare, use, start, blocks, buffers, then, every):
        whole = (blocks + 1) // 2
        here, there = buffers
        double = (whole - 1) // 2

        def step(i, carry):
            b = start + 4 * i
            together(use(b, 2, here), prepare(b + 2, there), every)
            together(use(b + 2, 2, there), prepare(b + 4, here), every)
            return carry

        if double:
            lax.fori_loop(0, double, step, 0)
        if whole % 2 == 0:
            b = start + 4 * double
            together(use(b, 2, here), prepare(b + 2, there), every)
            here, there = there, here
        final = use(start + 2 * (whole - 1), 2 - blocks % 2, here)
        if whole == 1:
            run(final)
            run(then(there))
        else:
            together(final, then(there), every)
        return there, here

    def predict(field, start, blocks, finish):
        sources_of = [field, series0, series1]
        buffers = (turned0, turned1)
        run(turn(field, start, buffers[0]))
        for degree in range(NORDER - 1):

            def use(b, many, buffer, degree=degree):
                for i in range(many):

                    def load(d, q, i=i):
                        value = buffer[i, pl.ds(216 * d + 24 * q, 24), :]
                        return value[0:16], value[16:24]

                    value = yield from apply_jacobian(b + i, load)
                    if degree < NORDER - 2:
                        sources_of[degree + 1][b + i] = value
                    else:
                        finish(b + i, [field[b + i], series0[b + i], series1[b + i], value])

            def prepare(b, buffer, degree=degree):
                return turn(sources_of[degree], b, buffer)

            def then(buffer, degree=degree):
                if degree < NORDER - 2:
                    yield from turn(sources_of[degree + 1], start, buffer)

            buffers = alternate(prepare, use, start, blocks, buffers, then, 3)

    def weighted(factors, members):
        total = factors[0] * members[0]
        for factor, member in zip(factors[1:], members[1:]):
            total = total + factor * member
        return total

    def finish_first(b, members):
        first[b] = weighted(to_first, members)
        second[b] = weighted(to_slow, members)

    predict(present, 0, KEPT_BLOCKS, finish_first)

    for copy in moves:
        copy.wait()
    for i in range(SLAB // LANES):
        pack[pl.ds(LANES * i, LANES), :] = got[1, :, pl.ds(LANES * i, LANES)].T
    present[8] = pack[pl.ds(0, ROWS), :]
    info[8] = pack[pl.ds(ROWS, 24), :]
    for p in range(QN):
        for q in range(QN):
            jac[p, q, :, pl.ds(E_DEV, LANES)] = pack[pl.ds(208 + 3 * (9 * p + q), 3), :]
    pair_block(8, 0)

    which = lax.broadcasted_iota(jnp.int32, (16, LANES), 0)
    near = jnp.where(which < 4, which + 1, count + 3 - which)
    wanted_step = jnp.where(which < 8, near, jnp.where(which == 8, count // 2, -7)).astype(F32)
    row_f = which.astype(F32)
    me_f = (jnp.zeros((1, LANES), jnp.int32) + me).astype(F32)
    r, c = grid_of(LANES, 2 * LANES)
    sums = one_hot(r < c)

    def owners(b):
        link = info[b, pl.ds(14, 4), :]
        owner = jnp.floor((link + 0.5) * (1.0 / PARTITION_SLOTS))
        local = link - owner * PARTITION_SLOTS
        away = jnp.where(owner != me_f, info[b, pl.ds(22, 1), :], 0.0) > 0.5
        return owner, local, away

    def scan(b, carry):
        running, asked = carry
        owner, local, away = owners(b)
        step = owner - me_f
        step = jnp.where(step < 0.0, step + count, step)
        step = jnp.max(jnp.where(away, step, -1.0), axis=0, keepdims=True)
        spot = jnp.max(jnp.where(away, local, 0.0), axis=0, keepdims=True)
        hit = wanted_step == step
        member = jnp.where(hit, 1.0, 0.0)
        prefix = dot(member.astype(BF16), sums)
        place = jnp.where(hit, 32.0 * row_f + running + prefix[:, :LANES], 0.0)
        found = jnp.sum(member, axis=0, keepdims=True)
        place = jnp.sum(place, axis=0, keepdims=True) - (1.0 - found)
        high = jnp.floor(spot * 0.125)
        text = jnp.concatenate([high, spot - 8.0 * high, found, jnp.zeros((13, LANES), F32)], axis=0)
        rows = lax.broadcasted_iota(jnp.int32, (ASKS, LANES), 0).astype(F32)
        chosen = one_hot(rows == place)
        placed[b] = chosen
        asked = asked + dot_nt(text.astype(BF16), chosen)
        return running + prefix[:, LANES:], asked

    counted = (jnp.zeros((16, LANES), F32), jnp.zeros((16, ASKS), F32))
    for b in range(BLOCKS):
        counted = scan(b, counted)
    asked = counted[1]
    asked = jnp.where(asked[2:3] > 0.5, 8.0 * asked[0:1] + asked[1:2], -1.0)
    ask_out[...] = jnp.broadcast_to(asked, (8, ASKS))
    requests = []
    for i, step in enumerate(reach):
        copy = pltpu.make_async_remote_copy(
            src_ref=ask_out.at[:, pl.ds(LANES * (i // 4), LANES)],
            dst_ref=ask_in.at[i],
            send_sem=ask_send.at[i],
            recv_sem=ask_recv.at[i],
            device_id=device(step),
            device_id_type=MESH,
        )
        copy.start()
        requests.append(copy)

    predict(present, KEPT_BLOCKS, 2, finish_first)

    for copy in requests:
        copy.wait()
    asker = lax.broadcasted_iota(jnp.int32, (1, ASKS), 1) // REQ
    asked = jnp.full((1, ASKS), -1.0, F32)
    for i in range(len(reach)):
        answer = jnp.concatenate([ask_in[i, 0:1, :]] * (ASKS // LANES), axis=1)
        asked = jnp.where(asker == i, answer, asked)
    slots = lax.broadcasted_iota(jnp.int32, (KEEP, ASKS), 0).astype(F32)
    wanted[...] = one_hot(slots == asked)

    def exchange(field, turn_index):
        for b in range(KEPT_BLOCKS):
            high, low = split(field[b])
            sources[pl.ds(0, ROWS), pl.ds(LANES * b, LANES)] = high
            sources[pl.ds(192, ROWS), pl.ds(LANES * b, LANES)] = low
        answer = dot(sources[...], wanted[...])
        answer = answer[0:ROWS] + answer[192 : 192 + ROWS]
        answer = jnp.concatenate([answer, jnp.zeros((256 - ROWS, ASKS), F32)], axis=0)
        for i in range(ASKS // LANES):
            for j in range(2):
                answer_out[turn_index, pl.ds(LANES * i, LANES), pl.ds(LANES * j, LANES)] = answer[
                    LANES * j : LANES * (j + 1), LANES * i : LANES * (i + 1)
                ].T
        copies = []
        for i, step in enumerate(reach):
            part = pl.ds(REQ * i, REQ)
            copy = pltpu.make_async_remote_copy(
                src_ref=answer_out.at[turn_index, part],
                dst_ref=answer_in.at[turn_index, part],
                send_sem=answer_send.at[turn_index, i],
                recv_sem=answer_recv.at[turn_index, i],
                device_id=device(-step),
                device_id_type=MESH,
            )
            copy.start()
            copies.append(copy)
        return copies

    def table_block(b):
        codes = info[b, pl.ds(18, 4), :]
        kinds = lax.broadcasted_iota(jnp.int32, (16, LANES), 0).astype(F32)
        chosen = jnp.concatenate([one_hot(kinds == codes[f : f + 1]) for f in range(4)], axis=1)
        value = dot(table[...], jnp.concatenate([chosen, chosen], axis=0))
        for f in range(4):
            tables[4 * b + f] = value[:, LANES * f : LANES * (f + 1)]
            yield

    def mark_block(b):
        _, local, _ = owners(b)
        slots = lax.broadcasted_iota(jnp.int32, (KEEP, LANES), 0).astype(F32)
        for f in range(4):
            marks[b, :, pl.ds(LANES * f, LANES)] = one_hot(slots == local[f : f + 1])
            yield

    def receive(turn_index, copies):
        for copy in copies:
            copy.wait()
        for i in range(ASKS // LANES):
            for j in range(2):
                block = answer_in[turn_index, pl.ds(LANES * i, LANES), pl.ds(LANES * j, LANES)].T
                if j == 1:
                    block = block[0 : ROWS - LANES]
                high, low = split(block)
                arrived[pl.ds(LANES * j, block.shape[0]), pl.ds(LANES * i, LANES)] = high
                arrived[pl.ds(192 + LANES * j, block.shape[0]), pl.ds(LANES * i, LANES)] = low

    def gather(b, target):
        _, _, away = owners(b)
        other = dot(arrived[...], placed[b])
        other = other[0:ROWS] + other[192 : 192 + ROWS]
        yield
        for half in range(2):
            value = None
            for start in range(0, KEEP, 256):
                depth = pl.ds(start, min(256, KEEP - start))
                part = dot(sources[:, depth], marks[b, depth, pl.ds(256 * half, 256)])
                value = part if value is None else value + part
                yield
            value = value[0:ROWS] + value[192 : 192 + ROWS]
            for i in range(2):
                f = 2 * half + i
                target[f] = jnp.where(away[f : f + 1], other, value[:, LANES * i : LANES * (i + 1)])
                yield

    def evaluate(b, outer):
        for f in range(4):
            i = 4 * b + f
            total = [points[i, pl.ds(NQ * q, NQ), :] for q in range(QN)]
            for c in range(BN):
                column = tables[i, pl.ds(NQ * c, NQ), :]
                for q in range(QN):
                    row = 16 * q + c if c < 16 else TAIL + 4 * q + c - 16
                    total[q] = total[q] + outer[f, pl.ds(row, 1), :] * column
                yield
            for q in range(QN):
                points[i, pl.ds(NQ * q, NQ), :] = total[q]

    def inside(field, b):
        for group in range(3):
            right = quad_rows(field, b, group)
            yield
            tall = 96 if group < 2 else 24
            wide = 64 if group < 2 else 16
            result = dot(stiff4[...] if group < 2 else stiff1[...], right)
            yield
            for d in range(4):
                put(volume, b, 216 * d + 96 * group, result[tall * d : tall * (d + 1)])
            yield
            for f in range(4):
                part = result[4 * tall + wide * f : 4 * tall + wide * (f + 1)]
                for i in range(2):
                    points[4 * (b + i) + f, pl.ds(64 * group, wide), :] = part[
                        :, LANES * i : LANES * (i + 1)
                    ]
            yield

    def lift(b, target):
        for group in range(3):
            wide = 64 if group < 2 else 16
            for f in range(4):
                parts = [points[4 * (b + i) + f, pl.ds(64 * group, wide), :] for i in range(2)]
                right = triple(jnp.concatenate(parts, axis=1))
                yield
                left = lift4[f] if group < 2 else lift1[f]
                put(target, 0, 216 * f + 96 * group, dot(left, right))
                yield

    def change_of(b, face):
        def load(d, q):
            value = volume[b, pl.ds(216 * d + 24 * q, 24), :]
            for f in range(4):
                value = value - info[b, pl.ds(4 * d + f, 1), :] * face[pl.ds(216 * f + 24 * q, 24), :]
            return value[0:16], value[16:24]

        change = yield from apply_jacobian(b, load)
        skew = []
        for q in range(QN):
            value = volume[b, pl.ds(648 + 24 * q, 24), :]
            for f in range(4):
                value = value - face[pl.ds(216 * f + 24 * q, 24), :]
            skew.append(value)
            yield
        tails = [
            jnp.where(low_half, skew[2 * i][16:24], skew[min(2 * i + 1, 8)][16:24]) for i in range(5)
        ]
        skew = jnp.concatenate([s[0:16] for s in skew] + tails, axis=0)
        return change - info[b, pl.ds(12, 1), :] * skew

    def update(turn_index, copies, finish, later):
        receive(turn_index, copies)
        run(gather(0, gathered0))

        def step(i, carry):
            together(evaluate(2 * i, gathered0), gather(2 * i + 1, gathered1), 8)
            together(evaluate(2 * i + 1, gathered1), gather(2 * i + 2, gathered0), 8)
            return carry

        lax.fori_loop(0, BLOCKS // 2, step, 0)
        together(evaluate(BLOCKS - 1, gathered0), lift(0, faces0), 4)

        def use(b, many, face):
            for i in range(many):
                change = yield from change_of(b + i, face.at[i])
                finish(b + i, change)

        if not later:
            alternate(lift, use, 0, BLOCKS, (faces0, faces1), lambda buffer: iter(()), 3)
            return None
        rest = alternate(lift, use, 0, KEPT_BLOCKS, (faces0, faces1), lambda buffer: lift(KEPT_BLOCKS, buffer), 3)
        return use(KEPT_BLOCKS, 2, rest[0])

    copies = exchange(first, 0)

    def tables_and_inside(i):
        yield from table_block(2 * i)
        yield from table_block(2 * i + 1)
        yield from inside(first, 2 * i)

    def mark_pair(i):
        yield from mark_block(2 * i)
        yield from mark_block(2 * i + 1)

    def ready(i, carry):
        together(tables_and_inside(i), mark_pair(i), 2)
        return carry

    lax.fori_loop(0, BLOCKS // 2 + 1, ready, 0)

    def finish_middle(b, change):
        base[b] = present[b] + change

    rest = update(0, copies, finish_middle, True)

    def finish_second(b, members):
        quick = info[b, pl.ds(13, 1), :] < 0.5
        second[b] = jnp.where(quick, weighted(to_first, members), second[b])

    predict(base, 0, KEPT_BLOCKS, finish_second)
    copies = exchange(second, 1)
    run(rest)
    predict(base, KEPT_BLOCKS, 2, finish_second)

    def inside_pair(i, carry):
        run(inside(second, 2 * i))
        return carry

    lax.fori_loop(0, BLOCKS // 2 + 1, inside_pair, 0)

    def finish_last(b, change):
        value = jnp.where(info[b, pl.ds(22, 1), :] > 0.5, base[b] + change, 0.0)
        at = pl.ds(pl.multiple_of(b * LANES, LANES), LANES)
        for q in range(QN):
            out_ref[q, 0:16, at] = value[16 * q : 16 * q + 16]
            out_ref[q, 16:20, at] = value[TAIL + 4 * q : TAIL + 4 * q + 4]

    update(1, copies, finish_last, False)


def per_device(
    count,
    element_freedom_values,
    scaled_jacobian_matrices,
    outward_face_normals,
    largest_wave_speed,
    element_cluster_index,
    element_new_slot,
    neighbours,
    face_rotation_codes,
    deriv_mats,
    stiff_mats,
    face_eval,
    face_lift,
):
    vmem = pl.BlockSpec(memory_space=pltpu.VMEM)
    return pl.pallas_call(
        functools.partial(kernel, count),
        out_shape=jax.ShapeDtypeStruct((QN, BN, PARTITION_SLOTS), F32),
        in_specs=[vmem, pl.BlockSpec(memory_space=pl.ANY)] + [vmem] * 10,
        out_specs=vmem,
        scratch_shapes=[
            pltpu.VMEM((288, 240), BF16),
            pltpu.VMEM((3, 24, 96), BF16),
            pltpu.VMEM((640, 240), BF16),
            pltpu.VMEM((160, 96), BF16),
            pltpu.VMEM((4, 96, 192), BF16),
            pltpu.VMEM((4, 24, 48), BF16),
            pltpu.VMEM((BN * NQ, 32), BF16),
            pltpu.VMEM((QN, QN, 3, PARTITION_SLOTS), F32),
            pltpu.VMEM((BLOCKS, 27, 5, 8, LANES), F32),
            pltpu.VMEM((BLOCKS + 1, 24, LANES), F32),
            pltpu.VMEM((BLOCKS + 1, ROWS, LANES), F32),
            pltpu.VMEM((BLOCKS + 1, ROWS, LANES), F32),
            pltpu.VMEM((BLOCKS + 1, ROWS, LANES), F32),
            pltpu.VMEM((BLOCKS + 1, ROWS, LANES), F32),
            pltpu.VMEM((BLOCKS + 1, ROWS, LANES), F32),
            pltpu.VMEM((BLOCKS + 1, ROWS, LANES), F32),
            pltpu.VMEM((2, 648, LANES), F32),
            pltpu.VMEM((2, 648, LANES), F32),
            pltpu.VMEM((BLOCKS + 1, 864, LANES), F32),
            pltpu.VMEM((2, 864, LANES), F32),
            pltpu.VMEM((2, 864, LANES), F32),
            pltpu.VMEM((4 * BLOCKS + 4, TAIL, LANES), F32),
            pltpu.VMEM((4, ROWS, LANES), F32),
            pltpu.VMEM((4, ROWS, LANES), F32),
            pltpu.VMEM((4 * BLOCKS + 4, BN * NQ, LANES), F32),
            pltpu.VMEM((384, KEEP), BF16),
            pltpu.VMEM((BLOCKS + 1, KEEP, 4 * LANES), BF16),
            pltpu.VMEM((KEEP, ASKS), BF16),
            pltpu.VMEM((BLOCKS, ASKS, LANES), BF16),
            pltpu.VMEM((384, ASKS), BF16),
            pltpu.VMEM((SLAB, LANES), F32),
            pltpu.VMEM((2, LANES, SLAB), F32),
            pltpu.VMEM((8, ASKS), F32),
            pltpu.VMEM((9, 8, LANES), F32),
            pltpu.VMEM((2, ASKS, 256), F32),
            pltpu.VMEM((2, ASKS, 256), F32),
            pltpu.SemaphoreType.DMA,
            pltpu.SemaphoreType.DMA((GROUPS,)),
            pltpu.SemaphoreType.DMA((GROUPS,)),
            pltpu.SemaphoreType.DMA((9,)),
            pltpu.SemaphoreType.DMA((9,)),
            pltpu.SemaphoreType.DMA((2, 9)),
            pltpu.SemaphoreType.DMA((2, 9)),
        ],
        compiler_params=pltpu.CompilerParams(
            collective_id=0, has_side_effects=True, vmem_limit_bytes=56 << 20
        ),
    )(
        element_freedom_values,
        jnp.transpose(scaled_jacobian_matrices, (1, 2, 0, 3)),
        jnp.transpose(outward_face_normals, (1, 0, 2)),
        largest_wave_speed[None],
        element_cluster_index[None],
        element_new_slot[None],
        neighbours,
        face_rotation_codes,
        deriv_mats,
        stiff_mats,
        jnp.swapaxes(face_eval, 1, 2),
        face_lift,
    )


def solution(mesh):
    placed = (
        P(None, None, "dom"),
        P(None, None, None, "dom"),
        P(None, None, "dom"),
        P("dom"),
        P("dom"),
        P("dom"),
        P(None, "dom"),
        P(None, "dom"),
        P(),
        P(),
        P(),
        P(),
    )
    return jax.shard_map(
        functools.partial(per_device, mesh.shape["dom"]),
        mesh=mesh,
        in_specs=placed,
        out_specs=P(None, None, "dom"),
        check_vma=False,
    )
```
